512 devices in a mesh: lon: 32 (over x_hi, z, core), lat: 16 (over y, x_lo).
Axes of the slice: x: 4 (x_hi: 2, x_lo: 2; x = x_hi * 2 + x_lo), y: 8, z: 8, core: 2. Of those that a mesh axis runs over, the one named last changes fastest.
Arguments:
- sample_collection: float32 [17, 6, 128, 4096], P(None, None, 'lat', 'lon'), may hold values from -5.5 to 5.5
- obs_index: int32 [16, 32, 128], P('lat', 'lon'), may hold values from 0 to 1023, as said below
- obs_count: int32 [16, 32], P('lat', 'lon'), may hold values from 42 to 128
- obs_value: float32 [16, 32, 128], P('lat', 'lon'), may hold values from -5 to 5
- obs_weight: float32 [16, 32, 128], P('lat', 'lon'), may hold values from 8 to 128
Outputs:
- analysis: float32 [17, 6, 128, 4096], P(None, None, 'lat', 'lon')
- analysis_spread: float32 [17, 17], replicated
The draws below stay inside these ranges and needn't reach their ends.
Inputs may be any that keep to these rules, and one draw needn't show every extreme that they name: `obs_index`: cell number within the tile, row-major over its 8 x 128 cells; slots at or past the tile's count are ignored.
All inputs are finite; a program needn't handle non-finite values.
Results may differ from the reference program's by a relative error of at most 0.00021.
Values sent between devices are 32-bit elements; how exact they have to be, the bound alone decides.
No kernel may reach another device: no remote copies, remote signals or barrier semaphores. Data moves between devices by JAX's collectives and lax.ppermute only.
A program may use at most 64 MiB of HBM per device.

```python
import math
import jax
import jax.numpy as jnp
from jax import lax

UNCERTAINTY_DIRS = 16
MEMBERS = 17
FIELDS = 6
CX = 128
CY = 8
SUBSTEPS = 4
OBS_DEV = 128
NX = 4096
NY = 128
N_LON = 32
N_LAT = 16


def draw_sample_collection(key, part):
    key_base, key_common, key_rough = jax.random.split(key, 3)
    row_values = jnp.arange(NY, dtype=jnp.float32)
    scale = 0.3 * jnp.exp(math.log(3.0) * row_values / max(NY - 1, 1))
    scale = scale.reshape(1, 1, NY, 1)
    common = jax.random.truncated_normal(key_common, -3.0, 3.0, (MEMBERS, FIELDS, 1, 1), jnp.float32)
    base = 0.5 * jax.random.truncated_normal(key_base, -3.0, 3.0, (1, FIELDS, NY, NX), jnp.float32)
    rough = jax.random.truncated_normal(key_rough, -3.0, 3.0, (MEMBERS, FIELDS, NY, NX), jnp.float32)
    return base + scale * 0.7 * (common + rough)


def draw_obs_index(key, part):
    tiles = NY // CY * (NX // CX)
    key_cells, key_place = jax.random.split(jax.random.fold_in(key, 11))
    cells = jax.random.randint(key_cells, (tiles * OBS_DEV,), 0, CY * CX, jnp.int32)
    places = jax.random.permutation(key_place, tiles * OBS_DEV)
    cells = cells.at[places[0]].set(CY * CX - 1)
    cells = cells.at[places[1]].set(0)
    return cells.reshape(NY // CY, NX // CX, OBS_DEV)


def draw_obs_count(key, part):
    tiles = NY // CY * (NX // CX)
    least = OBS_DEV // 3
    key_level, key_each, key_place = jax.random.split(jax.random.fold_in(key, 23), 3)
    level = jax.random.randint(key_level, (), least, OBS_DEV + 1, jnp.int32)
    raw_bits = jax.random.randint(key_each, (tiles,), 0, 1 << 20, jnp.int32)
    counts = least + raw_bits % (level - least + 1)
    places = jax.random.permutation(key_place, tiles)
    counts = counts.at[places[0]].set(OBS_DEV)
    counts = counts.at[places[1]].set(least)
    return counts.reshape(NY // CY, NX // CX)


def draw_obs_value(key, part):
    tiles_lat = NY // CY
    tiles_lon = NX // CX
    key_shift, key_noise = jax.random.split(jax.random.fold_in(key, 37))
    shift = jax.random.uniform(key_shift, (), jnp.float32, -2.0, 2.0)
    noise = jax.random.truncated_normal(key_noise, -3.0, 3.0, (tiles_lat, tiles_lon, OBS_DEV), jnp.float32)
    return noise + shift


def steps_of(key, extent, shards, low, high):
    factor_of, own = 1.0, jax.random.fold_in(key, 6)
    for position, blocks in shards:
        steps = jnp.exp(jax.random.uniform(jax.random.fold_in(own, position), (blocks,), jnp.float32, low / len(shards), high / len(shards)))
        factor_of = factor_of * jnp.repeat(steps, extent[position] // blocks).reshape([-1 if axis == position else 1 for axis in range(len(extent))])
    return factor_of


def setup_inputs(seed: int = 0) -> dict:
    key_of = jax.random.split(jax.random.key(seed), 6)
    return {
        "sample_collection": draw_sample_collection(jax.random.fold_in(key_of[5], 71), 0),
        "obs_index": draw_obs_index(jax.random.fold_in(key_of[5], 71), 0),
        "obs_count": draw_obs_count(jax.random.fold_in(key_of[5], 71), 0),
        "obs_value": draw_obs_value(jax.random.fold_in(key_of[5], 71), 0),
        "obs_weight": jnp.clip(jnp.exp(math.log(128.0) - 2.7725887 * jax.random.uniform(key_of[4], (N_LAT, N_LON, OBS_DEV), jnp.float32) ** steps_of(key_of[4], (N_LAT, N_LON, OBS_DEV), ((0, 16), (1, 32)), -0.2, 0.2)), 8.0, 128.0),
    }


time_step = 0.15
coriolis_scale = 0.5
grav_low = 0.5
depth_top = 4.0
depth_low = 6.0
forget = 0.9
highest = lax.Precision.HIGHEST

def from_east(quantity):
    return quantity[..., 1:-1, 2:]

def from_west(quantity):
    return quantity[..., 1:-1, :-2]

def from_north(quantity):
    return quantity[..., 2:, 1:-1]

def from_south(quantity):
    return quantity[..., :-2, 1:-1]

def neighbour_mean(quantity):
    return 0.25 * (from_east(quantity) + from_west(quantity) + from_north(quantity) + from_south(quantity))

def zonal_slope(quantity):
    return 0.5 * (from_east(quantity) - from_west(quantity))

def merid_slope(quantity):
    return 0.5 * (from_north(quantity) - from_south(quantity))

def layer_update(thick, zonal, merid, pressure, rest_depth, coriolis):
    column = rest_depth + thick
    thick_new = neighbour_mean(thick) - time_step * (zonal_slope(column * zonal) + merid_slope(column * merid))
    zonal_here = zonal[..., 1:-1, 1:-1]
    merid_here = merid[..., 1:-1, 1:-1]
    zonal_new = neighbour_mean(zonal) - time_step * (zonal_here * zonal_slope(zonal) + merid_here * merid_slope(zonal) - coriolis * merid_here + zonal_slope(pressure))
    merid_new = neighbour_mean(merid) - time_step * (zonal_here * zonal_slope(merid) + merid_here * merid_slope(merid) + coriolis * zonal_here + merid_slope(pressure))
    return (thick_new, zonal_new, merid_new)

def advance(padded, coriolis):
    thick_top = padded[..., 0, :, :]
    thick_low = padded[..., 3, :, :]
    press_top = thick_top + thick_low
    press_low = press_top + grav_low * thick_low
    upper_layer = layer_update(thick_top, padded[..., 1, :, :], padded[..., 2, :, :], press_top, depth_top, coriolis)
    lower_layer = layer_update(thick_low, padded[..., 4, :, :], padded[..., 5, :, :], press_low, depth_low, coriolis)
    return jnp.stack(upper_layer + lower_layer, axis=-3)

def coriolis_rows(first_row, row_count, total_rows):
    row_values = first_row + jnp.arange(row_count, dtype=jnp.float32)
    return (coriolis_scale * (2.0 * (row_values + 0.5) / total_rows - 1.0)).reshape(row_count, 1)

def mode_space(obs_gram, obs_proj):
    identity = jnp.eye(UNCERTAINTY_DIRS, dtype=jnp.float32)
    gamma_matrix = identity - 1.0 / MEMBERS
    precision = UNCERTAINTY_DIRS / forget * gamma_matrix + obs_gram
    factor = jnp.linalg.cholesky(precision)
    weights = jax.scipy.linalg.cho_solve((factor, True), obs_proj)
    projector = jnp.concatenate([identity, jnp.zeros((1, UNCERTAINTY_DIRS), jnp.float32)], axis=0) - 1.0 / MEMBERS
    root_fix = identity + (math.sqrt(MEMBERS) - 1.0) / UNCERTAINTY_DIRS
    omega_matrix = jnp.dot(projector, root_fix, precision=highest)
    rotation = math.sqrt(UNCERTAINTY_DIRS) * jax.scipy.linalg.solve_triangular(factor.T, omega_matrix.T, lower=False)
    return (weights, rotation)

def reference(sample_collection, obs_index, obs_count, obs_value, obs_weight):
    coriolis = coriolis_rows(0.0, NY, NY)

    def sample_prediction(single_sample):
        for substep in range(SUBSTEPS):
            wrapped = jnp.concatenate([single_sample[..., -1:], single_sample, single_sample[..., :1]], axis=-1)
            padded = jnp.pad(wrapped, ((0, 0), (1, 1), (0, 0)))
            single_sample = advance(padded, coriolis)
        return single_sample
    prediction_integration = lax.map(sample_prediction, sample_collection)
    sample_average_vector = lax.optimization_barrier(jnp.mean(prediction_integration, axis=0))
    uncertainty_directions = prediction_integration[:UNCERTAINTY_DIRS] - sample_average_vector
    mode_gram = jnp.zeros((UNCERTAINTY_DIRS, UNCERTAINTY_DIRS), jnp.float32)
    for quantity in range(FIELDS):
        flat = uncertainty_directions[:, quantity].reshape(UNCERTAINTY_DIRS, -1)
        mode_gram = mode_gram + jnp.dot(flat, flat.T, precision=highest)
    interface_elevation = prediction_integration[:, 0] + prediction_integration[:, 3]
    tile_lat = jnp.arange(N_LAT, dtype=jnp.int32).reshape(N_LAT, 1, 1)
    tile_lon = jnp.arange(N_LON, dtype=jnp.int32).reshape(1, N_LON, 1)
    obs_rows = tile_lat * CY + obs_index // CX
    obs_columns = tile_lon * CX + obs_index % CX
    observed = interface_elevation[:, obs_rows, obs_columns].reshape(MEMBERS, -1)
    live_slots = (jnp.arange(OBS_DEV, dtype=jnp.int32).reshape(1, 1, OBS_DEV) < obs_count[:, :, None]).astype(jnp.float32)
    weight = (obs_weight * live_slots / (OBS_DEV * N_LAT * N_LON)).reshape(-1)
    obs_mean = lax.optimization_barrier(jnp.mean(observed, axis=0))
    anomaly = observed[:UNCERTAINTY_DIRS] - obs_mean
    innovation = obs_value.reshape(-1) - obs_mean
    weighted = anomaly * weight
    obs_gram = jnp.dot(weighted, anomaly.T, precision=highest)
    obs_proj = jnp.dot(weighted, innovation, precision=highest)
    weights, rotation = mode_space(obs_gram, obs_proj)
    coefficient = weights[:, None] + rotation
    pieces = []
    for quantity in range(FIELDS):
        flat = uncertainty_directions[:, quantity].reshape(UNCERTAINTY_DIRS, -1)
        update = jnp.dot(coefficient.T, flat, precision=highest).reshape(MEMBERS, NY, NX)
        pieces.append(sample_average_vector[quantity] + update)
    analysis = jnp.stack(pieces, axis=1)
    spread = jnp.dot(rotation.T, jnp.dot(mode_gram, rotation, precision=highest), precision=highest) / (FIELDS * NY * NX)
    return (analysis, spread)
```

```python
import math

import jax
import jax.numpy as jnp
from jax import lax
from jax.experimental import pallas as pl
from jax.experimental.pallas import tpu as pltpu
from jax.sharding import PartitionSpec as P


DIRS = 16
MEMBERS = 17
FIELDS = 6
PAIRS = MEMBERS * FIELDS
SUBSTEPS = 4
RIM = 4
ROWS = 8
COLS = 128
CELLS = FIELDS * ROWS * COLS
STRIPS = FIELDS + 1

time_step = 0.15
depth_top = 4.0
depth_low = 6.0
forget = 0.9
highest = lax.Precision.HIGHEST
f32 = jnp.float32


def iota(shape, axis):
    return lax.broadcasted_iota(jnp.int32, shape, axis)


def vmem(count):
    return [pl.BlockSpec(memory_space=pltpu.VMEM)] * count


def pack_kernel(x_ref, north_ref, south_ref, strip_ref):
    lane = iota((ROWS, COLS), 1)
    for pair in range(PAIRS):
        block = x_ref[pair]
        north_ref[RIM * pair : RIM * (pair + 1), :] = block[RIM:, :]
        south_ref[RIM * pair : RIM * (pair + 1), :] = block[:RIM, :]
    for strip in range(STRIPS):
        total = jnp.zeros((ROWS, COLS), f32)
        for place in range(DIRS if strip < FIELDS else FIELDS):
            pair = place * FIELDS + strip if strip < FIELDS else DIRS * FIELDS + place
            moved = pltpu.roll(x_ref[pair], 8 * place, 1) if place else x_ref[pair]
            mask = ((lane - (8 * place - 4)) & (COLS - 1)) < 8
            total = jnp.where(mask, moved, total)
        strip_ref[strip] = total


def layer(thick, zonal, merid, slope_x, slope_y, depth, turn):
    (h, hE, hW, hN, hS), (u, uE, uW, uN, uS), (v, vE, vW, vN, vS) = thick, zonal, merid
    half = 0.5 * time_step
    flux = ((depth + hE) * uE - (depth + hW) * uW) + ((depth + hN) * vN - (depth + hS) * vS)
    h_new = 0.25 * ((hE + hW) + (hN + hS)) - half * flux
    u_new = 0.25 * ((uE + uW) + (uN + uS)) - (
        half * (u * (uE - uW) + v * (uN - uS) + slope_x) - turn * v
    )
    v_new = 0.25 * ((vE + vW) + (vN + vS)) - (
        half * (u * (vE - vW) + v * (vN - vS) + slope_y) + turn * u
    )
    return h_new, u_new, v_new


def advance(center, east, west, turn):
    stencil = []
    for c, e, w in zip(center, east, west):
        stencil.append((c, e, w, pltpu.roll(c, 15, 0), pltpu.roll(c, 1, 0)))
    top, low = stencil[0], stencil[3]
    top_x, top_y = top[1] - top[2], top[3] - top[4]
    low_x, low_y = low[1] - low[2], low[3] - low[4]
    sum_x, sum_y = top_x + low_x, top_y + low_y
    upper = layer(top, stencil[1], stencil[2], sum_x, sum_y, depth_top, turn)
    lower = layer(low, stencil[4], stencil[5], sum_x + 0.5 * low_x, sum_y + 0.5 * low_y, depth_low, turn)
    return upper + lower


def forecast_kernel(
    lat_ref, count_ref, x_ref, nm_ref, sm_ref, own_ref, cn_ref, cs_ref, index_ref, value_ref, weight_ref,
    modes_ref, pay_ref, state, strips, inner, dev, seen,
):
    lat = lat_ref[0, 0]
    lats = lat_ref[0, 1]
    tiles = lat_ref[0, 2]
    sub = iota((16, COLS), 0)
    lane = iota((16, COLS), 1)
    row = jnp.where(sub < 12, sub, sub - 16) + lat * ROWS
    inside = (row >= 0) & (row < lats * ROWS)
    turn = time_step * (0.5 * (2.0 * (row.astype(f32) + 0.5) / (lats * ROWS).astype(f32) - 1.0))
    sub8 = iota((ROWS, COLS), 0)

    for pair in range(PAIRS):
        state[0, pair, 0:8, :] = x_ref[pair]
        state[0, pair, 8:12, :] = nm_ref[RIM * pair : RIM * (pair + 1), :]
        state[0, pair, 12:16, :] = sm_ref[RIM * pair : RIM * (pair + 1), :]
    for strip in range(STRIPS):
        rim = jnp.where(sub8 < RIM, cn_ref[strip], cs_ref[strip])
        block = jnp.concatenate([own_ref[strip], rim], axis=0)
        if strip < FIELDS:
            strips[0, 0, strip] = block
        else:
            for field in range(FIELDS):
                strips[0, 1, field] = pltpu.roll(block, COLS - 8 * field, 1) if field else block

    for step in range(SUBSTEPS):
        now, later = step % 2, (step + 1) % 2

        def member_step(member, carry, now=now, later=later):
            which = member // DIRS
            place = member - which * DIRS
            shift = place * 8
            back = lax.rem(COLS - shift, COLS)
            edge = ((lane - shift + 1) & (COLS - 1)) < 2
            center, east, west = [], [], []
            for field in range(FIELDS):
                block = state[now, member * FIELDS + field]
                beyond = pltpu.roll(strips[now, which, field], back, 1)
                center.append(block)
                east.append(pltpu.roll(jnp.where(lane == 0, beyond, block), COLS - 1, 1))
                west.append(pltpu.roll(jnp.where(lane == COLS - 1, beyond, block), 1, 1))
                inner[which, field] = jnp.where(edge, pltpu.roll(block, shift, 1), inner[which, field])
            new = advance(center, east, west, turn)
            for field in range(FIELDS):
                state[later, member * FIELDS + field] = jnp.where(inside, new[field], 0.0)
            return carry

        lax.fori_loop(0, MEMBERS, member_step, 0)
        if step < SUBSTEPS - 1:
            for which in range(2):
                center, east, west = [], [], []
                for field in range(FIELDS):
                    block, beyond = strips[now, which, field], inner[which, field]
                    center.append(block)
                    east.append(pltpu.roll(jnp.where((lane & 7) == 0, beyond, block), COLS - 1, 1))
                    west.append(pltpu.roll(jnp.where((lane & 7) == 7, beyond, block), 1, 1))
                new = advance(center, east, west, turn)
                for field in range(FIELDS):
                    strips[later, which, field] = jnp.where(inside, new[field], 0.0)

    last = SUBSTEPS % 2
    cell = index_ref[...]
    column = jnp.broadcast_to(cell & (COLS - 1), (ROWS, COLS))
    at_row = jnp.broadcast_to(lax.shift_right_logical(cell, 7), (ROWS, COLS)) == sub8
    for member in range(MEMBERS):
        surface = state[last, member * FIELDS, 0:8, :] + state[last, member * FIELDS + 3, 0:8, :]
        picked = jnp.take_along_axis(surface, column, axis=1)
        seen[member : member + 1, :] = jnp.sum(jnp.where(at_row, picked, 0.0), axis=0, keepdims=True)

    for field in range(FIELDS):
        total = state[last, field, 0:8, :]
        for member in range(1, MEMBERS):
            total = total + state[last, member * FIELDS + field, 0:8, :]
        mean = total * (1.0 / MEMBERS)
        for member in range(DIRS):
            at = (member * FIELDS + field) * ROWS
            dev[at : at + ROWS, :] = state[last, member * FIELDS + field, 0:8, :] - mean
        at = (DIRS * FIELDS + field) * ROWS
        dev[at : at + ROWS, :] = mean
    for tile in range(FIELDS * ROWS):
        modes_ref[:, COLS * tile : COLS * (tile + 1)] = dev[pl.ds(tile, MEMBERS, stride=FIELDS * ROWS), :]

    modes = modes_ref[0:DIRS, :]
    mode_gram = lax.dot_general(modes, modes, (((1,), (1,)), ((), ())), precision=highest, preferred_element_type=f32)

    observed = seen[...]
    slot = iota((1, COLS), 1)
    live = (slot < count_ref[0, 0]).astype(f32)
    weight = weight_ref[...] * live / (COLS * tiles).astype(f32)
    obs_mean = jnp.sum(observed, axis=0, keepdims=True) * (1.0 / MEMBERS)
    anomaly = observed[0:DIRS, :] - obs_mean
    innovation = value_ref[...] - obs_mean
    weighted = anomaly * weight
    obs_gram = lax.dot_general(
        weighted, anomaly, (((1,), (1,)), ((), ())), precision=highest, preferred_element_type=f32
    )
    obs_proj = jnp.sum(weighted * innovation, axis=1, keepdims=True)
    pay_ref[...] = jnp.zeros((ROWS, COLS), f32)
    for half in range(2):
        rows, at = slice(8 * half, 8 * half + 8), 64 * half
        pay_ref[:, at : at + DIRS] = mode_gram[rows, :]
        pay_ref[:, at + DIRS : at + 2 * DIRS] = obs_gram[rows, :]
        pay_ref[:, at + 2 * DIRS : at + 2 * DIRS + 1] = obs_proj[rows, :]


def analysis_kernel(omega_ref, parts_ref, modes_ref, out_ref, spread_ref, cells):
    total = jnp.sum(parts_ref[...], axis=0)
    joined = jnp.concatenate([total[:, 0:64], total[:, 64:128]], axis=0)
    mode_gram = joined[:, 0:DIRS]
    sub = iota((DIRS, COLS), 0)
    lane = iota((DIRS, COLS), 1)
    work = jnp.concatenate([joined[:, DIRS:], jnp.zeros((DIRS, COLS - 48), f32)], axis=1)
    work = jnp.where(lane < DIRS + 1, work, 0.0)
    gamma = jnp.where(sub == lane, 1.0, 0.0) - 1.0 / MEMBERS
    work = work + jnp.where(lane < DIRS, (DIRS / forget) * gamma, 0.0)
    work = work + jnp.where(lane == sub + 2 * DIRS, 1.0, 0.0)
    for pivot in range(DIRS):
        column = jnp.broadcast_to(work[:, pivot : pivot + 1], (DIRS, COLS))
        inverse = 1.0 / jnp.sqrt(column[pivot : pivot + 1, :])
        row = work[pivot : pivot + 1, :] * inverse
        work = jnp.where(sub == pivot, row, work - jnp.where(sub > pivot, column * inverse, 0.0) * row)
    inverse_factor = work[:, 2 * DIRS : 3 * DIRS]
    solved = work[:, DIRS : DIRS + 1]
    weights = jnp.sum(solved * inverse_factor, axis=0, keepdims=True)
    rotation_t = jnp.dot(omega_ref[...], inverse_factor, precision=highest, preferred_element_type=f32)
    coefficient_t = rotation_t + weights
    for field in range(FIELDS):
        span = slice(field * ROWS * COLS, (field + 1) * ROWS * COLS)
        update = jnp.dot(coefficient_t, modes_ref[0:DIRS, span], precision=highest, preferred_element_type=f32)
        update = update + modes_ref[DIRS : DIRS + 1, span]
        for row_here in range(ROWS):
            cells[pl.ds(field * ROWS + row_here, MEMBERS, stride=FIELDS * ROWS), :] = update[
                :, COLS * row_here : COLS * (row_here + 1)
            ]
    out_ref[...] = cells[...].reshape(PAIRS, ROWS, COLS)
    half_way = jnp.dot(rotation_t, mode_gram, precision=highest, preferred_element_type=f32)
    spread_ref[...] = lax.dot_general(
        half_way, rotation_t, (((1,), (1,)), ((), ())), precision=highest, preferred_element_type=f32
    )


def omega():
    projector = [[(1.0 if i == j else 0.0) - 1.0 / MEMBERS for j in range(DIRS)] for i in range(MEMBERS)]
    root = (math.sqrt(MEMBERS) - 1.0) / DIRS
    rows = [[math.sqrt(DIRS) * (r[j] + root * sum(r)) for j in range(DIRS)] for r in projector]
    return jnp.array(rows, f32)


def sum_over(axis, part):
    count = lax.axis_size(axis)
    return lax.all_to_all(jnp.broadcast_to(part[None], (count,) + part.shape), axis, 0, 0)


def on_device(sample_collection, obs_index, obs_count, obs_value, obs_weight):
    lat_tiles, lon_tiles = lax.axis_size("lat"), lax.axis_size("lon")
    small = pltpu.CompilerParams(vmem_limit_bytes=12 * 2**20)
    blocks = sample_collection.reshape(PAIRS, ROWS, COLS)
    north_msg, south_msg, strip_msg = pl.pallas_call(
        pack_kernel,
        out_shape=[jax.ShapeDtypeStruct((PAIRS * RIM, COLS), f32)] * 2
        + [jax.ShapeDtypeStruct((STRIPS, ROWS, COLS), f32)],
        in_specs=vmem(1),
        out_specs=vmem(3),
        compiler_params=small,
    )(blocks)
    to_north = [(i, i + 1) for i in range(lat_tiles - 1)]
    to_south = [(j, i) for i, j in to_north]
    to_east = [(i, (i + 1) % lon_tiles) for i in range(lon_tiles)]
    to_west = [(j, i) for i, j in to_east]
    south_rows = lax.ppermute(north_msg, "lat", to_north)
    north_rows = lax.ppermute(south_msg, "lat", to_south)
    west_strip = lax.ppermute(strip_msg, "lon", to_east)
    east_strip = lax.ppermute(strip_msg, "lon", to_west)
    eastern = (iota(strip_msg.shape, 2) & 7) < RIM
    own_strip = jnp.where(eastern, east_strip, west_strip)
    south_strip = lax.ppermute(own_strip, "lat", to_north)
    north_strip = lax.ppermute(own_strip, "lat", to_south)

    scalars = jnp.stack([lax.axis_index("lat"), jnp.int32(lat_tiles), jnp.int32(lat_tiles * lon_tiles)]).reshape(1, 3)
    smem = pl.BlockSpec(memory_space=pltpu.SMEM)
    modes, part = pl.pallas_call(
        forecast_kernel,
        out_shape=[jax.ShapeDtypeStruct((MEMBERS, CELLS), f32), jax.ShapeDtypeStruct((ROWS, COLS), f32)],
        in_specs=[smem, smem] + vmem(9),
        out_specs=vmem(2),
        compiler_params=small,
        scratch_shapes=[
            pltpu.VMEM((2, PAIRS, 16, COLS), f32),
            pltpu.VMEM((2, 2, FIELDS, 16, COLS), f32),
            pltpu.VMEM((2, FIELDS, 16, COLS), f32),
            pltpu.VMEM((PAIRS * ROWS, COLS), f32),
            pltpu.VMEM((MEMBERS, COLS), f32),
        ],
    )(
        scalars, obs_count, blocks, north_rows, south_rows, own_strip, north_strip, south_strip,
        obs_index.reshape(1, COLS), obs_value.reshape(1, COLS), obs_weight.reshape(1, COLS),
    )
    part = jnp.sum(sum_over("lat", part), axis=0)
    parts = sum_over("lon", part)
    analysis, spread = pl.pallas_call(
        analysis_kernel,
        out_shape=[jax.ShapeDtypeStruct((PAIRS, ROWS, COLS), f32), jax.ShapeDtypeStruct((MEMBERS, MEMBERS), f32)],
        in_specs=vmem(3),
        out_specs=vmem(2),
        compiler_params=small,
        scratch_shapes=[pltpu.VMEM((PAIRS * ROWS, COLS), f32)],
    )(omega(), parts, modes)
    return analysis.reshape(sample_collection.shape), spread / (CELLS * lat_tiles * lon_tiles)


def solution(mesh):
    return jax.shard_map(
        on_device,
        mesh=mesh,
        in_specs=(
            P(None, None, "lat", "lon"),
            P("lat", "lon", None),
            P("lat", "lon"),
            P("lat", "lon", None),
            P("lat", "lon", None),
        ),
        out_specs=(P(None, None, "lat", "lon"), P()),
        check_vma=False,
    )
```

```python
import math

import jax
import jax.numpy as jnp
from jax import lax
from jax.experimental import pallas as pl
from jax.experimental.pallas import tpu as pltpu
from jax.sharding import PartitionSpec as P


DIRS = 16
MEMBERS = 17
FIELDS = 6
PAIRS = MEMBERS * FIELDS
SUBSTEPS = 4
RIM = 4
ROWS = 8
COLS = 128
CELLS = FIELDS * ROWS * COLS
TILES = FIELDS * ROWS
HOME = 12
DEEP = 32
GROUP = 2
STRIPS = FIELDS + 1

time_step = 0.15
depth_top = 4.0
depth_low = 6.0
forget = 0.9
highest = lax.Precision.HIGHEST
f32 = jnp.float32


def iota(shape, axis):
    return lax.broadcasted_iota(jnp.int32, shape, axis)


def vmem(count):
    return [pl.BlockSpec(memory_space=pltpu.VMEM)] * count


def pack_kernel(
    x_hbm, index_hbm, count_hbm, value_hbm, weight_hbm, first_ref, second_ref, strip_ref, obs_ref,
    x_ref, index_ref, count_ref, value_ref, weight_ref, sems,
):
    moves = [
        pltpu.make_async_copy(source, target, sems.at[place])
        for place, (source, target) in enumerate(
            [
                (x_hbm, x_ref),
                (index_hbm, index_ref),
                (count_hbm, count_ref),
                (value_hbm, value_ref),
                (weight_hbm, weight_ref),
            ]
        )
    ]
    for move in moves:
        move.start()
    for move in moves:
        move.wait()
    even = (lax.axis_index("lat") & 1) == 0
    tiles = lax.axis_size("lat") * lax.axis_size("lon")

    def rows_out(north_first):
        first, second = (slice(RIM, ROWS), slice(0, RIM)) if north_first else (slice(0, RIM), slice(RIM, ROWS))
        for pair in range(PAIRS):
            first_ref[RIM * pair : RIM * (pair + 1), :] = x_ref[pair, first, :]
            second_ref[RIM * pair : RIM * (pair + 1), :] = x_ref[pair, second, :]

    pl.when(even)(lambda: rows_out(True))
    pl.when(jnp.logical_not(even))(lambda: rows_out(False))
    lane = iota((ROWS, COLS), 1)
    for strip in range(STRIPS):
        total = jnp.zeros((ROWS, COLS), f32)
        for place in range(DIRS if strip < FIELDS else FIELDS):
            pair = place * FIELDS + strip if strip < FIELDS else DIRS * FIELDS + place
            moved = pltpu.roll(x_ref[pair], 8 * place, 1) if place else x_ref[pair]
            mask = ((lane - (8 * place - 4)) & (COLS - 1)) < 8
            total = jnp.where(mask, moved, total)
        strip_ref[strip] = total
    live = (iota((1, COLS), 1) < count_ref[...]).astype(f32)
    obs_ref[...] = jnp.zeros((ROWS, COLS), f32)
    obs_ref[0:1, :] = index_ref[...].astype(f32)
    obs_ref[1:2, :] = value_ref[...]
    obs_ref[2:3, :] = weight_ref[...] * live / float(COLS * tiles)


def layer(thick, zonal, merid, slope_x, slope_y, depth, turn):
    (h, hE, hW, hN, hS), (u, uE, uW, uN, uS), (v, vE, vW, vN, vS) = thick, zonal, merid
    half = 0.5 * time_step
    flux = ((depth + hE) * uE - (depth + hW) * uW) + ((depth + hN) * vN - (depth + hS) * vS)
    h_new = 0.25 * ((hE + hW) + (hN + hS)) - half * flux
    u_new = 0.25 * ((uE + uW) + (uN + uS)) - (
        half * (u * (uE - uW) + v * (uN - uS) + slope_x) - turn * v
    )
    v_new = 0.25 * ((vE + vW) + (vN + vS)) - (
        half * (u * (vE - vW) + v * (vN - vS) + slope_y) + turn * u
    )
    return h_new, u_new, v_new


def advance(stencil, turn):
    top, low = stencil[0], stencil[3]
    top_x, top_y = top[1] - top[2], top[3] - top[4]
    low_x, low_y = low[1] - low[2], low[3] - low[4]
    sum_x, sum_y = top_x + low_x, top_y + low_y
    upper = layer(top, stencil[1], stencil[2], sum_x, sum_y, depth_top, turn)
    lower = layer(low, stencil[4], stencil[5], sum_x + 0.5 * low_x, sum_y + 0.5 * low_y, depth_low, turn)
    return upper + lower


def split(value):
    high = value.astype(jnp.bfloat16)
    rest = value - high.astype(f32)
    middle = rest.astype(jnp.bfloat16)
    return high, middle, (rest - middle.astype(f32)).astype(jnp.bfloat16)


def forecast_kernel(
    x_ref, first_ref, second_ref, own_ref, rim1_ref, rim2_ref, obs_ref,
    modes_ref, mean_ref, pay_ref, state, state2, strips, strips2, inner, final, dev, seen, gram,
):
    lat = lax.axis_index("lat")
    lats = lax.axis_size("lat")
    even = (lat & 1) == 0

    def rows_in(north_first):
        north, south = (first_ref, second_ref) if north_first else (second_ref, first_ref)
        for pair in range(PAIRS):
            state[pair, HOME - RIM : HOME, :] = south[RIM * pair : RIM * (pair + 1), :]
            state[pair, HOME : HOME + ROWS, :] = x_ref[pair]
            state[pair, HOME + ROWS : HOME + ROWS + RIM, :] = north[RIM * pair : RIM * (pair + 1), :]
        north, south = (rim1_ref, rim2_ref) if north_first else (rim2_ref, rim1_ref)
        for strip in range(STRIPS):
            blocks = [south[strip], own_ref[strip], north[strip]]
            for field in range(FIELDS) if strip == FIELDS else [strip]:
                which = 1 if strip == FIELDS else 0
                if which and field:
                    low, mid, high = [pltpu.roll(block, COLS - 8 * field, 1) for block in blocks]
                else:
                    low, mid, high = blocks
                strips[which, field, HOME - RIM : HOME, :] = low[RIM:, :]
                strips[which, field, HOME : HOME + ROWS, :] = mid
                strips[which, field, HOME + ROWS : HOME + ROWS + RIM, :] = high[:RIM, :]

    pl.when(even)(lambda: rows_in(True))
    pl.when(jnp.logical_not(even))(lambda: rows_in(False))

    def row_terms(first):
        row = iota((ROWS, COLS), 0) + (first + lat * ROWS)
        inside = (row >= 0) & (row < lats * ROWS)
        turn = time_step * (0.5 * (2.0 * (row.astype(f32) + 0.5) / float(lats * ROWS) - 1.0))
        return inside, turn

    lane = iota((ROWS, COLS), 1)
    for step in range(SUBSTEPS):
        done = step == SUBSTEPS - 1
        old, fresh = (state, state2) if step % 2 == 0 else (state2, state)
        old_strips, fresh_strips = (strips, strips2) if step % 2 == 0 else (strips2, strips)
        starts = [HOME] if done else [HOME - RIM, HOME + RIM]

        def triple(ref, start, *at):
            return [ref[(*at, slice(start + d, start + d + ROWS), slice(None))] for d in (0, 1, -1)]

        def members_step(members, which, shifts):
            for half, start in enumerate(starts):
                inside, turn = row_terms(start - HOME)
                stencils = []
                for member, shift in zip(members, shifts):
                    stencil = []
                    for field in range(FIELDS):
                        c, n, s = triple(old, start, member * FIELDS + field)
                        beyond = old_strips[which, field, start : start + ROWS, :]
                        if shift is not None:
                            beyond = pltpu.roll(beyond, COLS - shift, 1)
                        e = pltpu.roll(jnp.where(lane == 0, beyond, c), COLS - 1, 1)
                        w = pltpu.roll(jnp.where(lane == COLS - 1, beyond, c), 1, 1)
                        stencil.append((c, e, w, n, s))
                    stencils.append(stencil)
                if not done:
                    for field in range(FIELDS):
                        if shifts[0] is None:
                            inner[which, field, ROWS * half : ROWS * (half + 1), :] = stencils[0][field][0]
                            continue
                        total = inner[which, field, ROWS * half : ROWS * (half + 1), :]
                        for shift, stencil in zip(shifts, stencils):
                            edge = ((lane - shift + 1) & (COLS - 1)) < 2
                            total = jnp.where(edge, pltpu.roll(stencil[field][0], shift, 1), total)
                        inner[which, field, ROWS * half : ROWS * (half + 1), :] = total
                for member, stencil in zip(members, stencils):
                    new = advance(stencil, turn)
                    for field in range(FIELDS):
                        if done:
                            final[member * FIELDS + field] = new[field]
                        else:
                            fresh[member * FIELDS + field, start : start + ROWS, :] = jnp.where(inside, new[field], 0.0)

        def group_step(index, carry):
            members = [GROUP * index + k for k in range(GROUP)]
            members_step(members, 0, [8 * member for member in members])
            return carry

        lax.fori_loop(0, DIRS // GROUP, group_step, 0)
        members_step([DIRS], 1, [None])
        if not done:
            for which in range(2):
                for half, start in enumerate(starts):
                    inside, turn = row_terms(start - HOME)
                    stencil = []
                    for field in range(FIELDS):
                        c, n, s = triple(old_strips, start, which, field)
                        beyond = inner[which, field, ROWS * half : ROWS * (half + 1), :]
                        e = pltpu.roll(jnp.where((lane & 7) == 0, beyond, c), COLS - 1, 1)
                        w = pltpu.roll(jnp.where((lane & 7) == 7, beyond, c), 1, 1)
                        stencil.append((c, e, w, n, s))
                    new = advance(stencil, turn)
                    for field in range(FIELDS):
                        fresh_strips[which, field, start : start + ROWS, :] = jnp.where(inside, new[field], 0.0)

    sub8 = iota((ROWS, COLS), 0)
    cell = obs_ref[0:1, :].astype(jnp.int32)
    column = jnp.broadcast_to(cell & (COLS - 1), (ROWS, COLS))
    at_row = jnp.broadcast_to(lax.shift_right_logical(cell, 7), (ROWS, COLS)) == sub8
    for member in range(MEMBERS):
        surface = final[member * FIELDS] + final[member * FIELDS + 3]
        picked = jnp.take_along_axis(surface, column, axis=1)
        seen[member : member + 1, :] = jnp.sum(jnp.where(at_row, picked, 0.0), axis=0, keepdims=True)

    for field in range(FIELDS):
        total = final[field]
        for member in range(1, MEMBERS):
            total = total + final[member * FIELDS + field]
        mean = total * (1.0 / MEMBERS)
        mean_ref[ROWS * field : ROWS * (field + 1), :] = mean
        for member in range(DIRS):
            at = member * TILES + field * ROWS
            dev[at : at + ROWS, :] = final[member * FIELDS + field] - mean
    for tile in range(TILES):
        span = slice(COLS * tile, COLS * (tile + 1))
        parts = split(dev[pl.ds(tile, DIRS, stride=TILES), :])
        for place, part in enumerate((0, 1, 2, 0, 1, 0)):
            modes_ref[DIRS * place : DIRS * (place + 1), span] = parts[part]

    stack = modes_ref[0 : 3 * DIRS, :]
    blocks = lax.dot_general(stack, stack, (((1,), (1,)), ((), ())), preferred_element_type=f32)
    rows3 = blocks[0:DIRS, :] + (blocks[DIRS : 2 * DIRS, :] + blocks[2 * DIRS :, :])
    mode_gram = rows3[:, 0:DIRS] + (rows3[:, DIRS : 2 * DIRS] + rows3[:, 2 * DIRS :])

    observed = seen[...]
    obs_mean = jnp.sum(observed, axis=0, keepdims=True) * (1.0 / MEMBERS)
    anomaly = observed[0:DIRS, :] - obs_mean
    innovation = obs_ref[1:2, :] - obs_mean
    weighted = anomaly * obs_ref[2:3, :]
    obs_gram = lax.dot_general(
        weighted, anomaly, (((1,), (1,)), ((), ())), precision=highest, preferred_element_type=f32
    )
    obs_proj = jnp.sum(weighted * innovation, axis=1, keepdims=True)
    row, col = iota((DIRS, DIRS), 0), iota((DIRS, DIRS), 1)
    gram[...] = jnp.zeros((DIRS, COLS), f32)
    gram[:, 0:DIRS] = jnp.where(row < col, obs_gram, mode_gram)
    gram[:, DIRS : DIRS + 1] = jnp.sum(jnp.where(row == col, obs_gram, 0.0), axis=1, keepdims=True)
    gram[:, DIRS + 1 : DIRS + 2] = obs_proj
    packed = gram[0:4, :]
    for quarter in range(1, 4):
        packed = packed + pltpu.roll(gram[4 * quarter : 4 * quarter + 4, :], 32 * quarter, 1)
    pay_ref[...] = packed


def analysis_kernel(parts_ref, modes_ref, mean_ref, out_ref, spread_ref, gram):
    packed = jnp.sum(parts_ref[...], axis=0)
    for quarter in range(4):
        gram[4 * quarter : 4 * quarter + 4, :] = (
            pltpu.roll(packed, COLS - 32 * quarter, 1) if quarter else packed
        )
    joined = gram[...]
    row, col = iota((DIRS, DIRS), 0), iota((DIRS, DIRS), 1)
    square = joined[:, 0:DIRS]
    upper = jnp.where(row < col, square, 0.0)
    lower = jnp.where(row > col, square, 0.0)
    mode_gram = jnp.where(row == col, square, 0.0) + (lower + lower.T)
    obs_gram = jnp.where(row == col, joined[:, DIRS : DIRS + 1], 0.0) + (upper + upper.T)
    precision = obs_gram + (DIRS / forget) * (jnp.where(row == col, 1.0, 0.0) - 1.0 / MEMBERS)
    sub, lane = iota((DIRS, COLS), 0), iota((DIRS, COLS), 1)
    copies = 6 * DIRS
    gram[:, copies : copies + DIRS] = precision
    gram[:, copies + DIRS : copies + DIRS + 1] = joined[:, DIRS + 1 : DIRS + 2]
    unit = jnp.where((lane & (DIRS - 1)) == sub, 1.0, 0.0)
    work = jnp.where(lane < copies, unit, gram[...])
    work = jnp.where(lane <= copies + DIRS, work, 0.0)
    for pivot in range(DIRS):
        column = jnp.broadcast_to(work[:, copies + pivot : copies + pivot + 1], (DIRS, COLS))
        value = column[pivot : pivot + 1, :]
        inverse = lax.rsqrt(value)
        inverse = inverse * (1.5 - 0.5 * value * inverse * inverse)
        pivot_row = work[pivot : pivot + 1, :] * inverse
        work = jnp.where(sub == pivot, pivot_row, work - jnp.where(sub > pivot, column * inverse, 0.0) * pivot_row)
    inverse_factor = work[:, :copies]
    solved = work[:, copies + DIRS : copies + DIRS + 1]
    weights = jnp.sum(solved * inverse_factor, axis=0, keepdims=True)
    spare = (math.sqrt(MEMBERS) - 1.0) / DIRS
    scale = math.sqrt(DIRS)
    sums = jnp.sum(inverse_factor, axis=0, keepdims=True)
    rotation_t = jnp.concatenate(
        [
            scale * inverse_factor + (scale * (spare - 1.0) / MEMBERS) * sums,
            (-scale * (1.0 + DIRS * spare) / MEMBERS) * sums,
        ],
        axis=0,
    )
    coefficient_t = rotation_t + weights
    high, middle, low = split(coefficient_t)
    place = iota((MEMBERS, copies), 1)
    stack = jnp.where(place < 3 * DIRS, high.astype(f32), jnp.where(place < 5 * DIRS, middle.astype(f32), low.astype(f32)))
    stack = stack.astype(jnp.bfloat16)
    for field in range(FIELDS):
        span = slice(field * ROWS * COLS, (field + 1) * ROWS * COLS)
        update = jnp.dot(stack, modes_ref[:, span], preferred_element_type=f32)
        for row_here in range(ROWS):
            tile = field * ROWS + row_here
            out_ref[pl.ds(tile, MEMBERS, stride=TILES), :] = (
                update[:, COLS * row_here : COLS * (row_here + 1)] + mean_ref[tile : tile + 1, :]
            )
    rotation_t = rotation_t[:, 0:DIRS]
    half_way = jnp.dot(rotation_t, mode_gram, precision=highest, preferred_element_type=f32)
    spread = lax.dot_general(
        half_way, rotation_t, (((1,), (1,)), ((), ())), precision=highest, preferred_element_type=f32
    )
    spread_ref[...] = spread / float(CELLS * lax.axis_size("lat") * lax.axis_size("lon"))


def neighbours(axis, parity, wrap):
    count = lax.axis_size(axis)
    pairs = [(i, i + 1) for i in range(parity, count - 1, 2)]
    if wrap and parity:
        pairs.append((count - 1, 0))
    return pairs + [(j, i) for i, j in pairs]


def all_parts(part, groups):
    count = len(groups[0])
    return lax.all_to_all(
        jnp.broadcast_to(part[None], (count,) + part.shape), ("lon", "lat"), 0, 0, axis_index_groups=groups
    )


def on_device(sample_collection, obs_index, obs_count, obs_value, obs_weight):
    lat_tiles, lon_tiles = lax.axis_size("lat"), lax.axis_size("lon")
    small = pltpu.CompilerParams(vmem_limit_bytes=16 * 2**20)
    blocks = sample_collection.reshape(PAIRS, ROWS, COLS)
    rows_shape = jax.ShapeDtypeStruct((PAIRS * RIM, COLS), f32)
    strips_shape = jax.ShapeDtypeStruct((STRIPS, ROWS, COLS), f32)
    first_msg, second_msg, strip_msg, obs = pl.pallas_call(
        pack_kernel,
        out_shape=[rows_shape, rows_shape, strips_shape, jax.ShapeDtypeStruct((ROWS, COLS), f32)],
        in_specs=[pl.BlockSpec(memory_space=pltpu.HBM)] * 5,
        out_specs=vmem(4),
        scratch_shapes=[
            pltpu.VMEM((PAIRS, ROWS, COLS), f32),
            pltpu.VMEM((1, COLS), jnp.int32),
            pltpu.VMEM((1, 1), jnp.int32),
            pltpu.VMEM((1, COLS), f32),
            pltpu.VMEM((1, COLS), f32),
            pltpu.SemaphoreType.DMA((5,)),
        ],
        compiler_params=small,
    )(blocks, obs_index.reshape(1, COLS), obs_count, obs_value.reshape(1, COLS), obs_weight.reshape(1, COLS))
    strip1 = lax.ppermute(strip_msg, "lon", neighbours("lon", 0, True))
    strip2 = lax.ppermute(strip_msg, "lon", neighbours("lon", 1, True))
    first = lax.ppermute(first_msg, "lat", neighbours("lat", 0, False))
    second = lax.ppermute(second_msg, "lat", neighbours("lat", 1, False))
    eastern = (iota(strip_msg.shape, 2) & 7) < RIM
    own_strip = jnp.where(eastern == ((lax.axis_index("lon") & 1) == 0), strip1, strip2)
    rim1 = lax.ppermute(own_strip, "lat", neighbours("lat", 0, False))
    rim2 = lax.ppermute(own_strip, "lat", neighbours("lat", 1, False))

    modes, mean, part = pl.pallas_call(
        forecast_kernel,
        out_shape=[
            jax.ShapeDtypeStruct((6 * DIRS, CELLS), jnp.bfloat16),
            jax.ShapeDtypeStruct((TILES, COLS), f32),
            jax.ShapeDtypeStruct((4, COLS), f32),
        ],
        in_specs=vmem(7),
        out_specs=vmem(3),
        scratch_shapes=[
            pltpu.VMEM((PAIRS, DEEP, COLS), f32),
            pltpu.VMEM((PAIRS, DEEP, COLS), f32),
            pltpu.VMEM((2, FIELDS, DEEP, COLS), f32),
            pltpu.VMEM((2, FIELDS, DEEP, COLS), f32),
            pltpu.VMEM((2, FIELDS, ROWS + 2 * RIM, COLS), f32),
            pltpu.VMEM((PAIRS, ROWS, COLS), f32),
            pltpu.VMEM((DIRS * TILES, COLS), f32),
            pltpu.VMEM((MEMBERS, COLS), f32),
            pltpu.VMEM((DIRS, COLS), f32),
        ],
        compiler_params=small,
    )(blocks, first, second, own_strip, rim1, rim2, obs)

    fine = min(16, lon_tiles)
    index = [[lon * lat_tiles + lat for lat in range(lat_tiles)] for lon in range(lon_tiles)]
    near = [
        [index[base + k][lat] for k in range(fine)] for base in range(0, lon_tiles, fine) for lat in range(lat_tiles)
    ]
    far = [[index[lon][lat] for lon in range(k, lon_tiles, fine) for lat in range(lat_tiles)] for k in range(fine)]
    part = jnp.sum(all_parts(part, near), axis=0)
    parts = all_parts(part, far)
    analysis, spread = pl.pallas_call(
        analysis_kernel,
        out_shape=[jax.ShapeDtypeStruct((PAIRS * ROWS, COLS), f32), jax.ShapeDtypeStruct((MEMBERS, MEMBERS), f32)],
        in_specs=vmem(3),
        out_specs=vmem(2),
        scratch_shapes=[pltpu.VMEM((DIRS, COLS), f32)],
        compiler_params=small,
    )(parts, modes, mean)
    return analysis.reshape(sample_collection.shape), spread


def solution(mesh):
    return jax.shard_map(
        on_device,
        mesh=mesh,
        in_specs=(
            P(None, None, "lat", "lon"),
            P("lat", "lon", None),
            P("lat", "lon"),
            P("lat", "lon", None),
            P("lat", "lon", None),
        ),
        out_specs=(P(None, None, "lat", "lon"), P()),
        check_vma=False,
    )
```

```python
import math

import jax
import jax.numpy as jnp
from jax import lax
from jax.experimental import pallas as pl
from jax.experimental.pallas import tpu as pltpu
from jax.sharding import PartitionSpec as P


DIRS = 16
MEMBERS = 17
FIELDS = 6
PAIRS = MEMBERS * FIELDS
SUBSTEPS = 4
RIM = 4
ROWS = 8
COLS = 128
CELLS = FIELDS * ROWS * COLS
TILES = FIELDS * ROWS
HOME = 12
DEEP = 32
GROUP = 2
STRIPS = FIELDS + 1

time_step = 0.15
depth_top = 4.0
depth_low = 6.0
forget = 0.9
highest = lax.Precision.HIGHEST
f32 = jnp.float32


def iota(shape, axis):
    return lax.broadcasted_iota(jnp.int32, shape, axis)


def vmem(count):
    return [pl.BlockSpec(memory_space=pltpu.VMEM)] * count


def pack_kernel(x_hbm, first_ref, second_ref, strip_ref, x_ref, sem):
    move = pltpu.make_async_copy(x_hbm, x_ref, sem)
    move.start()
    move.wait()
    even = (lax.axis_index("lat") & 1) == 0

    def rows_out(north_first):
        first, second = (slice(RIM, ROWS), slice(0, RIM)) if north_first else (slice(0, RIM), slice(RIM, ROWS))
        for pair in range(PAIRS):
            first_ref[RIM * pair : RIM * (pair + 1), :] = x_ref[pair, first, :]
            second_ref[RIM * pair : RIM * (pair + 1), :] = x_ref[pair, second, :]

    pl.when(even)(lambda: rows_out(True))
    pl.when(jnp.logical_not(even))(lambda: rows_out(False))
    lane = iota((ROWS, COLS), 1)
    for strip in range(STRIPS):
        total = jnp.zeros((ROWS, COLS), f32)
        for place in range(DIRS if strip < FIELDS else FIELDS):
            pair = place * FIELDS + strip if strip < FIELDS else DIRS * FIELDS + place
            moved = pltpu.roll(x_ref[pair], 8 * place, 1) if place else x_ref[pair]
            mask = ((lane - (8 * place - 4)) & (COLS - 1)) < 8
            total = jnp.where(mask, moved, total)
        strip_ref[strip] = total


def layer(thick, zonal, merid, slope_x, slope_y, depth, turn):
    (h, hE, hW, hN, hS), (u, uE, uW, uN, uS), (v, vE, vW, vN, vS) = thick, zonal, merid
    half = 0.5 * time_step
    flux = ((depth + hE) * uE - (depth + hW) * uW) + ((depth + hN) * vN - (depth + hS) * vS)
    h_new = 0.25 * ((hE + hW) + (hN + hS)) - half * flux
    u_new = 0.25 * ((uE + uW) + (uN + uS)) - (
        half * (u * (uE - uW) + v * (uN - uS) + slope_x) - turn * v
    )
    v_new = 0.25 * ((vE + vW) + (vN + vS)) - (
        half * (u * (vE - vW) + v * (vN - vS) + slope_y) + turn * u
    )
    return h_new, u_new, v_new


def advance(stencil, turn):
    top, low = stencil[0], stencil[3]
    top_x, top_y = top[1] - top[2], top[3] - top[4]
    low_x, low_y = low[1] - low[2], low[3] - low[4]
    sum_x, sum_y = top_x + low_x, top_y + low_y
    upper = layer(top, stencil[1], stencil[2], sum_x, sum_y, depth_top, turn)
    lower = layer(low, stencil[4], stencil[5], sum_x + 0.5 * low_x, sum_y + 0.5 * low_y, depth_low, turn)
    return upper + lower


def split(value):
    high = value.astype(jnp.bfloat16)
    rest = value - high.astype(f32)
    middle = rest.astype(jnp.bfloat16)
    return high, middle, (rest - middle.astype(f32)).astype(jnp.bfloat16)


def forecast_kernel(
    x_ref, first_ref, second_ref, own_ref, rim1_ref, rim2_ref, count_ref, index_hbm, value_hbm, weight_hbm,
    modes_ref, mean_ref, pay_ref,
    state, state2, strips, strips2, inner, final, dev, seen, gram, index_ref, value_ref, weight_ref, sems,
):
    moves = [
        pltpu.make_async_copy(source, target, sems.at[place])
        for place, (source, target) in enumerate(
            [(index_hbm, index_ref), (value_hbm, value_ref), (weight_hbm, weight_ref)]
        )
    ]
    for move in moves:
        move.start()
    lat = lax.axis_index("lat")
    lats = lax.axis_size("lat")
    even = (lat & 1) == 0

    def rows_in(north_first):
        north, south = (first_ref, second_ref) if north_first else (second_ref, first_ref)
        for pair in range(PAIRS):
            state[pair, HOME - RIM : HOME, :] = south[RIM * pair : RIM * (pair + 1), :]
            state[pair, HOME : HOME + ROWS, :] = x_ref[pair]
            state[pair, HOME + ROWS : HOME + ROWS + RIM, :] = north[RIM * pair : RIM * (pair + 1), :]
        north, south = (rim1_ref, rim2_ref) if north_first else (rim2_ref, rim1_ref)
        for strip in range(STRIPS):
            blocks = [south[strip], own_ref[strip], north[strip]]
            for field in range(FIELDS) if strip == FIELDS else [strip]:
                which = 1 if strip == FIELDS else 0
                if which and field:
                    low, mid, high = [pltpu.roll(block, COLS - 8 * field, 1) for block in blocks]
                else:
                    low, mid, high = blocks
                strips[which, field, HOME - RIM : HOME, :] = low[RIM:, :]
                strips[which, field, HOME : HOME + ROWS, :] = mid
                strips[which, field, HOME + ROWS : HOME + ROWS + RIM, :] = high[:RIM, :]

    pl.when(even)(lambda: rows_in(True))
    pl.when(jnp.logical_not(even))(lambda: rows_in(False))

    def row_terms(first):
        row = iota((ROWS, COLS), 0) + (first + lat * ROWS)
        inside = (row >= 0) & (row < lats * ROWS)
        turn = time_step * (0.5 * (2.0 * (row.astype(f32) + 0.5) / float(lats * ROWS) - 1.0))
        return inside, turn

    lane = iota((ROWS, COLS), 1)
    for step in range(SUBSTEPS):
        done = step == SUBSTEPS - 1
        old, fresh = (state, state2) if step % 2 == 0 else (state2, state)
        old_strips, fresh_strips = (strips, strips2) if step % 2 == 0 else (strips2, strips)
        starts = [HOME] if done else [HOME - RIM, HOME + RIM]

        def triple(ref, start, *at):
            return [ref[(*at, slice(start + d, start + d + ROWS), slice(None))] for d in (0, 1, -1)]

        def members_step(members, which, shifts):
            for half, start in enumerate(starts):
                inside, turn = row_terms(start - HOME)
                stencils = []
                for member, shift in zip(members, shifts):
                    stencil = []
                    for field in range(FIELDS):
                        c, n, s = triple(old, start, member * FIELDS + field)
                        beyond = old_strips[which, field, start : start + ROWS, :]
                        if shift is not None:
                            beyond = pltpu.roll(beyond, COLS - shift, 1)
                        e = pltpu.roll(jnp.where(lane == 0, beyond, c), COLS - 1, 1)
                        w = pltpu.roll(jnp.where(lane == COLS - 1, beyond, c), 1, 1)
                        stencil.append((c, e, w, n, s))
                    stencils.append(stencil)
                if not done:
                    for field in range(FIELDS):
                        if shifts[0] is None:
                            inner[which, field, ROWS * half : ROWS * (half + 1), :] = stencils[0][field][0]
                            continue
                        total = inner[which, field, ROWS * half : ROWS * (half + 1), :]
                        for shift, stencil in zip(shifts, stencils):
                            edge = ((lane - shift + 1) & (COLS - 1)) < 2
                            total = jnp.where(edge, pltpu.roll(stencil[field][0], shift, 1), total)
                        inner[which, field, ROWS * half : ROWS * (half + 1), :] = total
                for member, stencil in zip(members, stencils):
                    new = advance(stencil, turn)
                    for field in range(FIELDS):
                        if done:
                            final[member * FIELDS + field] = new[field]
                        else:
                            fresh[member * FIELDS + field, start : start + ROWS, :] = jnp.where(inside, new[field], 0.0)

        def group_step(index, carry):
            members = [GROUP * index + k for k in range(GROUP)]
            members_step(members, 0, [8 * member for member in members])
            return carry

        lax.fori_loop(0, DIRS // GROUP, group_step, 0)
        members_step([DIRS], 1, [None])
        if not done:
            for which in range(2):
                for half, start in enumerate(starts):
                    inside, turn = row_terms(start - HOME)
                    stencil = []
                    for field in range(FIELDS):
                        c, n, s = triple(old_strips, start, which, field)
                        beyond = inner[which, field, ROWS * half : ROWS * (half + 1), :]
                        e = pltpu.roll(jnp.where((lane & 7) == 0, beyond, c), COLS - 1, 1)
                        w = pltpu.roll(jnp.where((lane & 7) == 7, beyond, c), 1, 1)
                        stencil.append((c, e, w, n, s))
                    new = advance(stencil, turn)
                    for field in range(FIELDS):
                        fresh_strips[which, field, start : start + ROWS, :] = jnp.where(inside, new[field], 0.0)

    sub8 = iota((ROWS, COLS), 0)
    for move in moves:
        move.wait()
    cell = index_ref[...]
    column = jnp.broadcast_to(cell & (COLS - 1), (ROWS, COLS))
    at_row = jnp.broadcast_to(lax.shift_right_logical(cell, 7), (ROWS, COLS)) == sub8
    for member in range(MEMBERS):
        surface = final[member * FIELDS] + final[member * FIELDS + 3]
        picked = jnp.take_along_axis(surface, column, axis=1)
        seen[member : member + 1, :] = jnp.sum(jnp.where(at_row, picked, 0.0), axis=0, keepdims=True)

    for field in range(FIELDS):
        total = final[field]
        for member in range(1, MEMBERS):
            total = total + final[member * FIELDS + field]
        mean = total * (1.0 / MEMBERS)
        mean_ref[ROWS * field : ROWS * (field + 1), :] = mean
        for member in range(DIRS):
            at = member * TILES + field * ROWS
            dev[at : at + ROWS, :] = final[member * FIELDS + field] - mean
    for tile in range(TILES):
        span = slice(COLS * tile, COLS * (tile + 1))
        parts = split(dev[pl.ds(tile, DIRS, stride=TILES), :])
        for place, part in enumerate((0, 1, 2, 0, 1, 0)):
            modes_ref[DIRS * place : DIRS * (place + 1), span] = parts[part]

    stack = modes_ref[0 : 3 * DIRS, :]
    blocks = lax.dot_general(stack, stack, (((1,), (1,)), ((), ())), preferred_element_type=f32)
    rows3 = blocks[0:DIRS, :] + (blocks[DIRS : 2 * DIRS, :] + blocks[2 * DIRS :, :])
    mode_gram = rows3[:, 0:DIRS] + (rows3[:, DIRS : 2 * DIRS] + rows3[:, 2 * DIRS :])

    observed = seen[...]
    obs_mean = jnp.sum(observed, axis=0, keepdims=True) * (1.0 / MEMBERS)
    anomaly = observed[0:DIRS, :] - obs_mean
    innovation = value_ref[...] - obs_mean
    live = (iota((1, COLS), 1) < count_ref[...]).astype(f32)
    weighted = anomaly * (weight_ref[...] * live / float(COLS * lats * lax.axis_size("lon")))
    obs_gram = lax.dot_general(
        weighted, anomaly, (((1,), (1,)), ((), ())), precision=highest, preferred_element_type=f32
    )
    obs_proj = jnp.sum(weighted * innovation, axis=1, keepdims=True)
    row, col = iota((DIRS, DIRS), 0), iota((DIRS, DIRS), 1)
    gram[...] = jnp.zeros((DIRS, COLS), f32)
    gram[:, 0:DIRS] = jnp.where(row < col, obs_gram, mode_gram)
    gram[:, DIRS : DIRS + 1] = jnp.sum(jnp.where(row == col, obs_gram, 0.0), axis=1, keepdims=True)
    gram[:, DIRS + 1 : DIRS + 2] = obs_proj
    packed = gram[0:4, :]
    for quarter in range(1, 4):
        packed = packed + pltpu.roll(gram[4 * quarter : 4 * quarter + 4, :], 32 * quarter, 1)
    pay_ref[...] = packed


def analysis_kernel(parts_ref, modes_ref, mean_ref, out_ref, spread_ref, gram):
    packed = jnp.sum(parts_ref[...], axis=0)
    for quarter in range(4):
        gram[4 * quarter : 4 * quarter + 4, :] = (
            pltpu.roll(packed, COLS - 32 * quarter, 1) if quarter else packed
        )
    joined = gram[...]
    row, col = iota((DIRS, DIRS), 0), iota((DIRS, DIRS), 1)
    square = joined[:, 0:DIRS]
    upper = jnp.where(row < col, square, 0.0)
    lower = jnp.where(row > col, square, 0.0)
    mode_gram = jnp.where(row == col, square, 0.0) + (lower + lower.T)
    obs_gram = jnp.where(row == col, joined[:, DIRS : DIRS + 1], 0.0) + (upper + upper.T)
    precision = obs_gram + (DIRS / forget) * (jnp.where(row == col, 1.0, 0.0) - 1.0 / MEMBERS)
    sub, lane = iota((DIRS, COLS), 0), iota((DIRS, COLS), 1)
    copies = 6 * DIRS
    gram[:, copies : copies + DIRS] = precision
    gram[:, copies + DIRS : copies + DIRS + 1] = joined[:, DIRS + 1 : DIRS + 2]
    unit = jnp.where((lane & (DIRS - 1)) == sub, 1.0, 0.0)
    work = jnp.where(lane < copies, unit, gram[...])
    work = jnp.where(lane <= copies + DIRS, work, 0.0)
    for pivot in range(DIRS):
        column = jnp.broadcast_to(work[:, copies + pivot : copies + pivot + 1], (DIRS, COLS))
        value = column[pivot : pivot + 1, :]
        inverse = lax.rsqrt(value)
        inverse = inverse * (1.5 - 0.5 * value * inverse * inverse)
        pivot_row = work[pivot : pivot + 1, :] * inverse
        work = jnp.where(sub == pivot, pivot_row, work - jnp.where(sub > pivot, column * inverse, 0.0) * pivot_row)
    inverse_factor = work[:, :copies]
    solved = work[:, copies + DIRS : copies + DIRS + 1]
    weights = jnp.sum(solved * inverse_factor, axis=0, keepdims=True)
    spare = (math.sqrt(MEMBERS) - 1.0) / DIRS
    scale = math.sqrt(DIRS)
    sums = jnp.sum(inverse_factor, axis=0, keepdims=True)
    rotation_t = jnp.concatenate(
        [
            scale * inverse_factor + (scale * (spare - 1.0) / MEMBERS) * sums,
            (-scale * (1.0 + DIRS * spare) / MEMBERS) * sums,
        ],
        axis=0,
    )
    coefficient_t = rotation_t + weights
    high, middle, low = split(coefficient_t)
    place = iota((MEMBERS, copies), 1)
    stack = jnp.where(place < 3 * DIRS, high.astype(f32), jnp.where(place < 5 * DIRS, middle.astype(f32), low.astype(f32)))
    stack = stack.astype(jnp.bfloat16)
    for field in range(FIELDS):
        span = slice(field * ROWS * COLS, (field + 1) * ROWS * COLS)
        update = jnp.dot(stack, modes_ref[:, span], preferred_element_type=f32)
        for row_here in range(ROWS):
            tile = field * ROWS + row_here
            out_ref[pl.ds(tile, MEMBERS, stride=TILES), :] = (
                update[:, COLS * row_here : COLS * (row_here + 1)] + mean_ref[tile : tile + 1, :]
            )
    rotation_t = rotation_t[:, 0:DIRS]
    half_way = jnp.dot(rotation_t, mode_gram, precision=highest, preferred_element_type=f32)
    spread = lax.dot_general(
        half_way, rotation_t, (((1,), (1,)), ((), ())), precision=highest, preferred_element_type=f32
    )
    spread_ref[...] = spread / float(CELLS * lax.axis_size("lat") * lax.axis_size("lon"))


def neighbours(axis, parity, wrap):
    count = lax.axis_size(axis)
    pairs = [(i, i + 1) for i in range(parity, count - 1, 2)]
    if wrap and parity:
        pairs.append((count - 1, 0))
    return pairs + [(j, i) for i, j in pairs]


def all_parts(part, groups):
    count = len(groups[0])
    return lax.all_to_all(
        jnp.broadcast_to(part[None], (count,) + part.shape), ("lon", "lat"), 0, 0, axis_index_groups=groups
    )


def on_device(sample_collection, obs_index, obs_count, obs_value, obs_weight):
    lat_tiles, lon_tiles = lax.axis_size("lat"), lax.axis_size("lon")
    small = pltpu.CompilerParams(vmem_limit_bytes=16 * 2**20)
    blocks = sample_collection.reshape(PAIRS, ROWS, COLS)
    rows_shape = jax.ShapeDtypeStruct((PAIRS * RIM, COLS), f32)
    strips_shape = jax.ShapeDtypeStruct((STRIPS, ROWS, COLS), f32)
    in_hbm = pl.BlockSpec(memory_space=pltpu.HBM)
    blocks, index, value, weight = [
        pltpu.with_memory_space_constraint(array, pltpu.HBM)
        for array in (
            blocks, obs_index.reshape(1, COLS), obs_value.reshape(1, COLS), obs_weight.reshape(1, COLS)
        )
    ]
    first_msg, second_msg, strip_msg, here = pl.pallas_call(
        pack_kernel,
        out_shape=[rows_shape, rows_shape, strips_shape, jax.ShapeDtypeStruct((PAIRS, ROWS, COLS), f32)],
        in_specs=[in_hbm],
        out_specs=vmem(4),
        scratch_shapes=[pltpu.SemaphoreType.DMA],
        compiler_params=small,
    )(blocks)
    strip1 = lax.ppermute(strip_msg, "lon", neighbours("lon", 0, True))
    strip2 = lax.ppermute(strip_msg, "lon", neighbours("lon", 1, True))
    first = lax.ppermute(first_msg, "lat", neighbours("lat", 0, False))
    second = lax.ppermute(second_msg, "lat", neighbours("lat", 1, False))
    eastern = (iota(strip_msg.shape, 2) & 7) < RIM
    own_strip = jnp.where(eastern == ((lax.axis_index("lon") & 1) == 0), strip1, strip2)
    rim1 = lax.ppermute(own_strip, "lat", neighbours("lat", 0, False))
    rim2 = lax.ppermute(own_strip, "lat", neighbours("lat", 1, False))

    modes, mean, part = pl.pallas_call(
        forecast_kernel,
        out_shape=[
            jax.ShapeDtypeStruct((6 * DIRS, CELLS), jnp.bfloat16),
            jax.ShapeDtypeStruct((TILES, COLS), f32),
            jax.ShapeDtypeStruct((4, COLS), f32),
        ],
        in_specs=vmem(7) + [in_hbm] * 3,
        out_specs=vmem(3),
        scratch_shapes=[
            pltpu.VMEM((PAIRS, DEEP, COLS), f32),
            pltpu.VMEM((PAIRS, DEEP, COLS), f32),
            pltpu.VMEM((2, FIELDS, DEEP, COLS), f32),
            pltpu.VMEM((2, FIELDS, DEEP, COLS), f32),
            pltpu.VMEM((2, FIELDS, ROWS + 2 * RIM, COLS), f32),
            pltpu.VMEM((PAIRS, ROWS, COLS), f32),
            pltpu.VMEM((DIRS * TILES, COLS), f32),
            pltpu.VMEM((MEMBERS, COLS), f32),
            pltpu.VMEM((DIRS, COLS), f32),
            pltpu.VMEM((1, COLS), jnp.int32),
            pltpu.VMEM((1, COLS), f32),
            pltpu.VMEM((1, COLS), f32),
            pltpu.SemaphoreType.DMA((3,)),
        ],
        compiler_params=small,
    )(
        here, first, second, own_strip, rim1, rim2, jnp.broadcast_to(obs_count, (1, COLS)), index, value, weight
    )

    fine = min(16, lon_tiles)
    index = [[lon * lat_tiles + lat for lat in range(lat_tiles)] for lon in range(lon_tiles)]
    near = [
        [index[base + k][lat] for k in range(fine)] for base in range(0, lon_tiles, fine) for lat in range(lat_tiles)
    ]
    far = [[index[lon][lat] for lon in range(k, lon_tiles, fine) for lat in range(lat_tiles)] for k in range(fine)]
    part = jnp.sum(all_parts(part, near), axis=0)
    parts = all_parts(part, far)
    analysis, spread = pl.pallas_call(
        analysis_kernel,
        out_shape=[jax.ShapeDtypeStruct((PAIRS * ROWS, COLS), f32), jax.ShapeDtypeStruct((MEMBERS, MEMBERS), f32)],
        in_specs=vmem(3),
        out_specs=vmem(2),
        scratch_shapes=[pltpu.VMEM((DIRS, COLS), f32)],
        compiler_params=small,
    )(parts, modes, mean)
    return analysis.reshape(sample_collection.shape), spread


def solution(mesh):
    return jax.shard_map(
        on_device,
        mesh=mesh,
        in_specs=(
            P(None, None, "lat", "lon"),
            P("lat", "lon", None),
            P("lat", "lon"),
            P("lat", "lon", None),
            P("lat", "lon", None),
        ),
        out_specs=(P(None, None, "lat", "lon"), P()),
        check_vma=False,
    )
```

```python
import math

import jax
import jax.numpy as jnp
from jax import lax
from jax.experimental import pallas as pl
from jax.experimental.pallas import tpu as pltpu
from jax.sharding import PartitionSpec as P


DIRS = 16
MEMBERS = 17
FIELDS = 6
PAIRS = MEMBERS * FIELDS
SUBSTEPS = 4
RIM = 4
ROWS = 8
COLS = 128
CELLS = FIELDS * ROWS * COLS
TILES = FIELDS * ROWS
HOME = 12
DEEP = 32
GUARD = 8
GROUP = 4
STRIPS = FIELDS + 1
MSG_ROWS = (PAIRS + STRIPS) * RIM

time_step = 0.15
depth_top = 4.0
depth_low = 6.0
forget = 0.9
highest = lax.Precision.HIGHEST
f32 = jnp.float32


def iota(shape, axis):
    return lax.broadcasted_iota(jnp.int32, shape, axis)


def vmem(count):
    return [pl.BlockSpec(memory_space=pltpu.VMEM)] * count


def pack_kernel(x_hbm, strip_ref, x_ref, sem):
    move = pltpu.make_async_copy(x_hbm, x_ref.at[:, GUARD : GUARD + ROWS, :], sem)
    move.start()
    move.wait()
    lane = iota((ROWS, COLS), 1)
    for strip in range(STRIPS):
        total = jnp.zeros((ROWS, COLS), f32)
        for place in range(DIRS if strip < FIELDS else FIELDS):
            pair = place * FIELDS + strip if strip < FIELDS else DIRS * FIELDS + place
            block = x_ref[pair, GUARD : GUARD + ROWS, :]
            moved = pltpu.roll(block, 8 * place, 1) if place else block
            mask = ((lane - (8 * place - 4)) & (COLS - 1)) < 8
            total = jnp.where(mask, moved, total)
        strip_ref[strip] = total


def message_kernel(x_ref, strip1_ref, strip2_ref, own_ref, first_ref, second_ref):
    even_lon = (lax.axis_index("lon") & 1) == 0
    even_lat = (lax.axis_index("lat") & 1) == 0
    eastern = (iota((ROWS, COLS), 1) & 7) < RIM

    def merge(first_is_east):
        east, west = (strip1_ref, strip2_ref) if first_is_east else (strip2_ref, strip1_ref)
        for strip in range(STRIPS):
            own_ref[strip] = jnp.where(eastern, east[strip], west[strip])

    pl.when(even_lon)(lambda: merge(True))
    pl.when(jnp.logical_not(even_lon))(lambda: merge(False))

    def rows_out(north_first):
        north, south = (first_ref, second_ref) if north_first else (second_ref, first_ref)
        for pair in range(PAIRS):
            at = slice(RIM * pair, RIM * (pair + 1))
            north[at, :] = x_ref[pair, GUARD + RIM : GUARD + ROWS, :]
            south[at, :] = x_ref[pair, GUARD : GUARD + RIM, :]
        for strip in range(STRIPS):
            at = slice(RIM * (PAIRS + strip), RIM * (PAIRS + strip + 1))
            north[at, :] = own_ref[strip, RIM:ROWS, :]
            south[at, :] = own_ref[strip, 0:RIM, :]

    pl.when(even_lat)(lambda: rows_out(True))
    pl.when(jnp.logical_not(even_lat))(lambda: rows_out(False))


def layer(thick, zonal, merid, slope_x, slope_y, depth, turn):
    (h, hE, hW, hN, hS), (u, uE, uW, uN, uS), (v, vE, vW, vN, vS) = thick, zonal, merid
    half = 0.5 * time_step
    flux = ((depth + hE) * uE - (depth + hW) * uW) + ((depth + hN) * vN - (depth + hS) * vS)
    h_new = 0.25 * ((hE + hW) + (hN + hS)) - half * flux
    u_new = 0.25 * ((uE + uW) + (uN + uS)) - (
        half * (u * (uE - uW) + v * (uN - uS) + slope_x) - turn * v
    )
    v_new = 0.25 * ((vE + vW) + (vN + vS)) - (
        half * (u * (vE - vW) + v * (vN - vS) + slope_y) + turn * u
    )
    return h_new, u_new, v_new


def advance(stencil, turn):
    top, low = stencil[0], stencil[3]
    top_x, top_y = top[1] - top[2], top[3] - top[4]
    low_x, low_y = low[1] - low[2], low[3] - low[4]
    sum_x, sum_y = top_x + low_x, top_y + low_y
    upper = layer(top, stencil[1], stencil[2], sum_x, sum_y, depth_top, turn)
    lower = layer(low, stencil[4], stencil[5], sum_x + 0.5 * low_x, sum_y + 0.5 * low_y, depth_low, turn)
    return upper + lower


def split(value):
    high = value.astype(jnp.bfloat16)
    rest = value - high.astype(f32)
    middle = rest.astype(jnp.bfloat16)
    return high, middle, (rest - middle.astype(f32)).astype(jnp.bfloat16)


def sweep(read, emit, read_strip, emit_strip, inner, turn):
    lane = iota((ROWS, COLS), 1)

    def members_step(members, which, shifts):
        stencils = []
        for member, shift in zip(members, shifts):
            stencil = []
            for field in range(FIELDS):
                c, n, s = read(member * FIELDS + field)
                beyond = read_strip(which, field)[0]
                if shift is not None:
                    beyond = pltpu.roll(beyond, COLS - shift, 1)
                e = pltpu.roll(jnp.where(lane == 0, beyond, c), COLS - 1, 1)
                w = pltpu.roll(jnp.where(lane == COLS - 1, beyond, c), 1, 1)
                stencil.append((c, e, w, n, s))
            stencils.append(stencil)
        if emit_strip is not None:
            for field in range(FIELDS):
                if shifts[0] is None:
                    inner[which, field] = stencils[0][field][0]
                    continue
                total = inner[which, field]
                for shift, stencil in zip(shifts, stencils):
                    edge = ((lane - shift + 1) & (COLS - 1)) < 2
                    total = jnp.where(edge, pltpu.roll(stencil[field][0], shift, 1), total)
                inner[which, field] = total
        for member, stencil in zip(members, stencils):
            for field, value in enumerate(advance(stencil, turn)):
                emit(member * FIELDS + field, value)

    def group_step(index, carry):
        members = [GROUP * index + k for k in range(GROUP)]
        members_step(members, 0, [8 * member for member in members])
        return carry

    lax.fori_loop(0, DIRS // GROUP, group_step, 0)
    members_step([DIRS], 1, [None])
    if emit_strip is None:
        return
    for which in range(2):
        stencil = []
        for field in range(FIELDS):
            c, n, s = read_strip(which, field)
            beyond = inner[which, field]
            e = pltpu.roll(jnp.where((lane & 7) == 0, beyond, c), COLS - 1, 1)
            w = pltpu.roll(jnp.where((lane & 7) == 7, beyond, c), 1, 1)
            stencil.append((c, e, w, n, s))
        for field, value in enumerate(advance(stencil, turn)):
            emit_strip(which, field, value)


def row_terms(first, second):
    lats = lax.axis_size("lat")
    sub = iota((ROWS, COLS), 0)
    row = jnp.where(sub < RIM, sub + first, sub - RIM + second) + lax.axis_index("lat") * ROWS
    inside = (row >= 0) & (row < lats * ROWS)
    turn = time_step * (0.5 * (2.0 * (row.astype(f32) + 0.5) / float(lats * ROWS) - 1.0))
    return inside, turn


def spread_strips(blocks, strips, first, last, at):
    for strip in range(STRIPS):
        for field in range(FIELDS) if strip == FIELDS else [strip]:
            block = blocks(strip)
            if strip == FIELDS and field:
                block = pltpu.roll(block, COLS - 8 * field, 1)
            strips[strip // FIELDS, field, at : at + last - first, :] = block[first:last, :]


def interior_kernel(x_ref, own_ref, *refs):
    levels, strip_levels, inner = [x_ref, *refs[0:3]], [refs[6], *refs[3:6]], refs[7]
    _, turn = row_terms(0, RIM)
    spread_strips(lambda strip: own_ref[strip], strip_levels[0], 0, ROWS, HOME)
    for step in range(SUBSTEPS - 1):
        old, fresh = levels[step], levels[step + 1]
        old_strips, fresh_strips = strip_levels[step], strip_levels[step + 1]

        def read(pair, old=old):
            return [old[pair, GUARD + d : GUARD + d + ROWS, :] for d in (0, 1, -1)]

        def emit(pair, value, fresh=fresh):
            fresh[pair, GUARD : GUARD + ROWS, :] = value

        def read_strip(which, field, old_strips=old_strips):
            return [old_strips[which, field, HOME + d : HOME + d + ROWS, :] for d in (0, 1, -1)]

        def emit_strip(which, field, value, fresh_strips=fresh_strips):
            fresh_strips[which, field, HOME : HOME + ROWS, :] = value

        sweep(read, emit, read_strip, emit_strip, inner, turn)


def forecast_kernel(
    x_ref, own_ref, inner1, inner2, inner3, strip1, strip2, strip3, first_ref, second_ref,
    count_ref, index_hbm, value_hbm, weight_hbm,
    modes_ref, mean_ref, pay_ref,
    state0, state1, state2, state3, strips0, strips1, strips2, strips3, inner, final, dev, seen, gram,
    index_ref, value_ref, weight_ref, sems,
):
    moves = [
        pltpu.make_async_copy(source, target, sems.at[place])
        for place, (source, target) in enumerate(
            [(index_hbm, index_ref), (value_hbm, value_ref), (weight_hbm, weight_ref)]
        )
    ]
    for move in moves:
        move.start()
    lats = lax.axis_size("lat")
    even = (lax.axis_index("lat") & 1) == 0
    states = [state0, state1, state2, state3]
    strips = [strips0, strips1, strips2, strips3]

    def rows_in(north_first):
        north, south = (first_ref, second_ref) if north_first else (second_ref, first_ref)
        for pair in range(PAIRS):
            at = slice(RIM * pair, RIM * (pair + 1))
            state0[pair, HOME - RIM : HOME, :] = south[at, :]
            state0[pair, HOME + ROWS : HOME + ROWS + RIM, :] = north[at, :]

        def corner(rows):
            return lambda strip: rows[RIM * (PAIRS + strip) : RIM * (PAIRS + strip + 1), :]

        spread_strips(corner(south), strips0, 0, RIM, HOME - RIM)
        spread_strips(corner(north), strips0, 0, RIM, HOME + ROWS)

    pl.when(even)(lambda: rows_in(True))
    pl.when(jnp.logical_not(even))(lambda: rows_in(False))
    home = slice(HOME, HOME + ROWS)
    for source, target in zip((x_ref, inner1, inner2, inner3), states):
        for pair in range(PAIRS):
            target[pair, home, :] = source[pair, GUARD : GUARD + ROWS, :]
    spread_strips(lambda strip: own_ref[strip], strips0, 0, ROWS, HOME)
    for source, target in zip((strip1, strip2, strip3), strips[1:]):
        for which in range(2):
            for field in range(FIELDS):
                target[which, field, home, :] = source[which, field, home, :]

    upper = iota((ROWS, COLS), 0) < RIM
    for step in range(SUBSTEPS - 1):
        low, high = step - 3, 7 - step
        inside, turn = row_terms(low, high)

        def both(ref, *at, low=low, high=high):
            return [
                jnp.where(
                    upper,
                    ref[(*at, slice(HOME + low + d, HOME + low + d + ROWS), slice(None))],
                    ref[(*at, slice(HOME + high - RIM + d, HOME + high + RIM + d), slice(None))],
                )
                for d in (0, 1, -1)
            ]

        def put(ref, value, *at, low=low, high=high, inside=inside):
            value = jnp.where(inside, value, 0.0)
            ref[(*at, slice(HOME + low, HOME + low + RIM), slice(None))] = value[0:RIM, :]
            ref[(*at, slice(HOME + high, HOME + high + RIM), slice(None))] = value[RIM:ROWS, :]

        sweep(
            lambda pair, step=step, both=both: both(states[step], pair),
            lambda pair, value, step=step, put=put: put(states[step + 1], value, pair),
            lambda which, field, step=step, both=both: both(strips[step], which, field),
            lambda which, field, value, step=step, put=put: put(strips[step + 1], value, which, field),
            inner,
            turn,
        )

    def own_rows(ref, *at):
        return [ref[(*at, slice(HOME + d, HOME + d + ROWS), slice(None))] for d in (0, 1, -1)]

    def finish(pair, value):
        final[pair] = value

    sweep(
        lambda pair: own_rows(state3, pair),
        finish,
        lambda which, field: own_rows(strips3, which, field),
        None,
        inner,
        row_terms(0, RIM)[1],
    )

    sub8 = iota((ROWS, COLS), 0)
    for move in moves:
        move.wait()
    cell = index_ref[...]
    column = jnp.broadcast_to(cell & (COLS - 1), (ROWS, COLS))
    at_row = jnp.broadcast_to(lax.shift_right_logical(cell, 7), (ROWS, COLS)) == sub8
    for member in range(MEMBERS):
        surface = final[member * FIELDS] + final[member * FIELDS + 3]
        picked = jnp.take_along_axis(surface, column, axis=1)
        seen[member : member + 1, :] = jnp.sum(jnp.where(at_row, picked, 0.0), axis=0, keepdims=True)

    for field in range(FIELDS):
        total = final[field]
        for member in range(1, MEMBERS):
            total = total + final[member * FIELDS + field]
        mean = total * (1.0 / MEMBERS)
        mean_ref[ROWS * field : ROWS * (field + 1), :] = mean
        for member in range(DIRS):
            at = member * TILES + field * ROWS
            dev[at : at + ROWS, :] = final[member * FIELDS + field] - mean
    for tile in range(TILES):
        span = slice(COLS * tile, COLS * (tile + 1))
        parts = split(dev[pl.ds(tile, DIRS, stride=TILES), :])
        for place, part in enumerate(parts):
            modes_ref[DIRS * place : DIRS * (place + 1), span] = part

    stack = modes_ref[...]
    blocks = lax.dot_general(stack, stack, (((1,), (1,)), ((), ())), preferred_element_type=f32)
    rows3 = blocks[0:DIRS, :] + (blocks[DIRS : 2 * DIRS, :] + blocks[2 * DIRS :, :])
    mode_gram = rows3[:, 0:DIRS] + (rows3[:, DIRS : 2 * DIRS] + rows3[:, 2 * DIRS :])

    observed = seen[...]
    obs_mean = jnp.sum(observed, axis=0, keepdims=True) * (1.0 / MEMBERS)
    anomaly = observed[0:DIRS, :] - obs_mean
    innovation = value_ref[...] - obs_mean
    live = (iota((1, COLS), 1) < count_ref[...]).astype(f32)
    weighted = anomaly * (weight_ref[...] * live / float(COLS * lats * lax.axis_size("lon")))
    obs_gram = lax.dot_general(
        weighted, anomaly, (((1,), (1,)), ((), ())), precision=highest, preferred_element_type=f32
    )
    obs_proj = jnp.sum(weighted * innovation, axis=1, keepdims=True)
    row, col = iota((DIRS, DIRS), 0), iota((DIRS, DIRS), 1)
    gram[...] = jnp.zeros((DIRS, COLS), f32)
    gram[:, 0:DIRS] = jnp.where(row < col, obs_gram, mode_gram)
    gram[:, DIRS : DIRS + 1] = jnp.sum(jnp.where(row == col, obs_gram, 0.0), axis=1, keepdims=True)
    gram[:, DIRS + 1 : DIRS + 2] = obs_proj
    packed = gram[0:4, :]
    for quarter in range(1, 4):
        packed = packed + pltpu.roll(gram[4 * quarter : 4 * quarter + 4, :], 32 * quarter, 1)
    pay_ref[...] = packed


def analysis_kernel(parts_ref, modes_ref, mean_ref, out_ref, spread_ref, gram):
    packed = jnp.sum(parts_ref[...], axis=0)
    for quarter in range(4):
        gram[4 * quarter : 4 * quarter + 4, :] = (
            pltpu.roll(packed, COLS - 32 * quarter, 1) if quarter else packed
        )
    joined = gram[...]
    row, col = iota((DIRS, DIRS), 0), iota((DIRS, DIRS), 1)
    square = joined[:, 0:DIRS]
    upper = jnp.where(row < col, square, 0.0)
    lower = jnp.where(row > col, square, 0.0)
    mode_gram = jnp.where(row == col, square, 0.0) + (lower + lower.T)
    obs_gram = jnp.where(row == col, joined[:, DIRS : DIRS + 1], 0.0) + (upper + upper.T)
    precision = obs_gram + (DIRS / forget) * (jnp.where(row == col, 1.0, 0.0) - 1.0 / MEMBERS)
    sub, lane = iota((DIRS, COLS), 0), iota((DIRS, COLS), 1)
    copies = 6 * DIRS
    gram[:, copies : copies + DIRS] = precision
    gram[:, copies + DIRS : copies + DIRS + 1] = joined[:, DIRS + 1 : DIRS + 2]
    unit = jnp.where((lane & (DIRS - 1)) == sub, 1.0, 0.0)
    work = jnp.where(lane < copies, unit, gram[...])
    work = jnp.where(lane <= copies + DIRS, work, 0.0)
    for pivot in range(DIRS):
        column = jnp.broadcast_to(work[:, copies + pivot : copies + pivot + 1], (DIRS, COLS))
        value = column[pivot : pivot + 1, :]
        inverse = lax.rsqrt(value)
        inverse = inverse * (1.5 - 0.5 * value * inverse * inverse)
        pivot_row = work[pivot : pivot + 1, :] * inverse
        work = jnp.where(sub == pivot, pivot_row, work - jnp.where(sub > pivot, column * inverse, 0.0) * pivot_row)
    inverse_factor = work[:, :copies]
    solved = work[:, copies + DIRS : copies + DIRS + 1]
    weights = jnp.sum(solved * inverse_factor, axis=0, keepdims=True)
    spare = (math.sqrt(MEMBERS) - 1.0) / DIRS
    scale = math.sqrt(DIRS)
    sums = jnp.sum(inverse_factor, axis=0, keepdims=True)
    rotation_t = jnp.concatenate(
        [
            scale * inverse_factor + (scale * (spare - 1.0) / MEMBERS) * sums,
            (-scale * (1.0 + DIRS * spare) / MEMBERS) * sums,
        ],
        axis=0,
    )
    coefficient_t = rotation_t + weights
    high, middle, low = split(coefficient_t)
    place = iota((MEMBERS, copies), 1)
    stack = jnp.where(place < 3 * DIRS, high.astype(f32), jnp.where(place < 5 * DIRS, middle.astype(f32), low.astype(f32)))
    stack = stack.astype(jnp.bfloat16)
    for field in range(FIELDS):
        span = slice(field * ROWS * COLS, (field + 1) * ROWS * COLS)
        parts = jnp.concatenate(
            [modes_ref[:, span], modes_ref[0 : 2 * DIRS, span], modes_ref[0:DIRS, span]], axis=0
        )
        update = jnp.dot(stack, parts, preferred_element_type=f32)
        for row_here in range(ROWS):
            tile = field * ROWS + row_here
            out_ref[pl.ds(tile, MEMBERS, stride=TILES), :] = (
                update[:, COLS * row_here : COLS * (row_here + 1)] + mean_ref[tile : tile + 1, :]
            )
    rotation_t = rotation_t[:, 0:DIRS]
    half_way = jnp.dot(rotation_t, mode_gram, precision=highest, preferred_element_type=f32)
    spread = lax.dot_general(
        half_way, rotation_t, (((1,), (1,)), ((), ())), precision=highest, preferred_element_type=f32
    )
    spread_ref[...] = spread / float(CELLS * lax.axis_size("lat") * lax.axis_size("lon"))


def neighbours(axis, parity, wrap):
    count = lax.axis_size(axis)
    pairs = [(i, i + 1) for i in range(parity, count - 1, 2)]
    if wrap and parity:
        pairs.append((count - 1, 0))
    return pairs + [(j, i) for i, j in pairs]


def all_parts(part, groups):
    count = len(groups[0])
    return lax.all_to_all(
        jnp.broadcast_to(part[None], (count,) + part.shape), ("lon", "lat"), 0, 0, axis_index_groups=groups
    )


def on_device(sample_collection, obs_index, obs_count, obs_value, obs_weight):
    lat_tiles, lon_tiles = lax.axis_size("lat"), lax.axis_size("lon")
    small = pltpu.CompilerParams(vmem_limit_bytes=20 * 2**20)
    in_hbm = pl.BlockSpec(memory_space=pltpu.HBM)
    blocks, index, value, weight = [
        pltpu.with_memory_space_constraint(array, pltpu.HBM)
        for array in (
            sample_collection.reshape(PAIRS, ROWS, COLS),
            obs_index.reshape(1, COLS),
            obs_value.reshape(1, COLS),
            obs_weight.reshape(1, COLS),
        )
    ]
    strips_shape = jax.ShapeDtypeStruct((STRIPS, ROWS, COLS), f32)
    level_shape = jax.ShapeDtypeStruct((PAIRS, ROWS + 2 * GUARD, COLS), f32)
    strip_level = (2, FIELDS, DEEP, COLS)
    strip_msg, here = pl.pallas_call(
        pack_kernel,
        out_shape=[strips_shape, level_shape],
        in_specs=[in_hbm],
        out_specs=vmem(2),
        scratch_shapes=[pltpu.SemaphoreType.DMA],
        compiler_params=small,
    )(blocks)
    strip1 = lax.ppermute(strip_msg, "lon", neighbours("lon", 0, True))
    strip2 = lax.ppermute(strip_msg, "lon", neighbours("lon", 1, True))
    own_strip, first_msg, second_msg = pl.pallas_call(
        message_kernel,
        out_shape=[strips_shape] + [jax.ShapeDtypeStruct((MSG_ROWS, COLS), f32)] * 2,
        in_specs=vmem(3),
        out_specs=vmem(3),
        compiler_params=small,
    )(here, strip1, strip2)
    first = lax.ppermute(first_msg, "lat", neighbours("lat", 0, False))
    second = lax.ppermute(second_msg, "lat", neighbours("lat", 1, False))
    interior = pl.pallas_call(
        interior_kernel,
        out_shape=[level_shape] * 3 + [jax.ShapeDtypeStruct(strip_level, f32)] * 3,
        in_specs=vmem(2),
        out_specs=vmem(6),
        scratch_shapes=[pltpu.VMEM(strip_level, f32), pltpu.VMEM((2, FIELDS, ROWS, COLS), f32)],
        compiler_params=small,
        cost_estimate=pl.CostEstimate(flops=40_000_000, bytes_accessed=2_000_000, transcendentals=0),
    )(here, own_strip)

    modes, mean, part = pl.pallas_call(
        forecast_kernel,
        out_shape=[
            jax.ShapeDtypeStruct((3 * DIRS, CELLS), jnp.bfloat16),
            jax.ShapeDtypeStruct((TILES, COLS), f32),
            jax.ShapeDtypeStruct((4, COLS), f32),
        ],
        in_specs=vmem(11) + [in_hbm] * 3,
        out_specs=vmem(3),
        scratch_shapes=[pltpu.VMEM((PAIRS, DEEP, COLS), f32)] * 4
        + [pltpu.VMEM(strip_level, f32)] * 4
        + [
            pltpu.VMEM((2, FIELDS, ROWS, COLS), f32),
            pltpu.VMEM((PAIRS, ROWS, COLS), f32),
            pltpu.VMEM((DIRS * TILES, COLS), f32),
            pltpu.VMEM((MEMBERS, COLS), f32),
            pltpu.VMEM((DIRS, COLS), f32),
            pltpu.VMEM((1, COLS), jnp.int32),
            pltpu.VMEM((1, COLS), f32),
            pltpu.VMEM((1, COLS), f32),
            pltpu.SemaphoreType.DMA((3,)),
        ],
        compiler_params=small,
    )(
        here, own_strip, *interior, first, second,
        jnp.broadcast_to(obs_count, (1, COLS)), index, value, weight,
    )

    fine = min(16, lon_tiles)
    index = [[lon * lat_tiles + lat for lat in range(lat_tiles)] for lon in range(lon_tiles)]
    near = [
        [index[base + k][lat] for k in range(fine)] for base in range(0, lon_tiles, fine) for lat in range(lat_tiles)
    ]
    far = [[index[lon][lat] for lon in range(k, lon_tiles, fine) for lat in range(lat_tiles)] for k in range(fine)]
    part = jnp.sum(all_parts(part, near), axis=0)
    parts = all_parts(part, far)
    analysis, spread = pl.pallas_call(
        analysis_kernel,
        out_shape=[jax.ShapeDtypeStruct((PAIRS * ROWS, COLS), f32), jax.ShapeDtypeStruct((MEMBERS, MEMBERS), f32)],
        in_specs=vmem(3),
        out_specs=vmem(2),
        scratch_shapes=[pltpu.VMEM((DIRS, COLS), f32)],
        compiler_params=small,
    )(parts, modes, mean)
    return analysis.reshape(sample_collection.shape), spread


def solution(mesh):
    return jax.shard_map(
        on_device,
        mesh=mesh,
        in_specs=(
            P(None, None, "lat", "lon"),
            P("lat", "lon", None),
            P("lat", "lon"),
            P("lat", "lon", None),
            P("lat", "lon", None),
        ),
        out_specs=(P(None, None, "lat", "lon"), P()),
        check_vma=False,
    )
```

```python
import math

import jax
import jax.numpy as jnp
from jax import lax
from jax.experimental import pallas as pl
from jax.experimental.pallas import tpu as pltpu
from jax.sharding import PartitionSpec as P


DIRS = 16
MEMBERS = 17
FIELDS = 6
PAIRS = MEMBERS * FIELDS
SUBSTEPS = 4
RIM = 4
ROWS = 8
COLS = 128
CELLS = FIELDS * ROWS * COLS
TILES = FIELDS * ROWS
HOME = 12
DEEP = 32
GROUP = 4
STRIPS = FIELDS + 1
MSG_ROWS = (PAIRS + STRIPS) * RIM

time_step = 0.15
depth_top = 4.0
depth_low = 6.0
forget = 0.9
highest = lax.Precision.HIGHEST
f32 = jnp.float32


def iota(shape, axis):
    return lax.broadcasted_iota(jnp.int32, shape, axis)


def vmem(count):
    return [pl.BlockSpec(memory_space=pltpu.VMEM)] * count


def pack_kernel(x_hbm, strip_ref, x_ref, sem):
    move = pltpu.make_async_copy(x_hbm, x_ref.at[:, HOME : HOME + ROWS, :], sem)
    move.start()
    move.wait()
    lane = iota((ROWS, COLS), 1)
    for strip in range(STRIPS):
        total = jnp.zeros((ROWS, COLS), f32)
        for place in range(DIRS if strip < FIELDS else FIELDS):
            pair = place * FIELDS + strip if strip < FIELDS else DIRS * FIELDS + place
            block = x_ref[pair, HOME : HOME + ROWS, :]
            moved = pltpu.roll(block, 8 * place, 1) if place else block
            mask = ((lane - (8 * place - 4)) & (COLS - 1)) < 8
            total = jnp.where(mask, moved, total)
        strip_ref[strip] = total


def message_kernel(x_ref, strip1_ref, strip2_ref, own_ref, first_ref, second_ref):
    even_lon = (lax.axis_index("lon") & 1) == 0
    even_lat = (lax.axis_index("lat") & 1) == 0
    eastern = (iota((ROWS, COLS), 1) & 7) < RIM

    def merge(first_is_east):
        east, west = (strip1_ref, strip2_ref) if first_is_east else (strip2_ref, strip1_ref)
        for strip in range(STRIPS):
            own_ref[strip] = jnp.where(eastern, east[strip], west[strip])

    pl.when(even_lon)(lambda: merge(True))
    pl.when(jnp.logical_not(even_lon))(lambda: merge(False))

    def rows_out(north_first):
        north, south = (first_ref, second_ref) if north_first else (second_ref, first_ref)
        for pair in range(PAIRS):
            at = slice(RIM * pair, RIM * (pair + 1))
            north[at, :] = x_ref[pair, HOME + RIM : HOME + ROWS, :]
            south[at, :] = x_ref[pair, HOME : HOME + RIM, :]
        for strip in range(STRIPS):
            at = slice(RIM * (PAIRS + strip), RIM * (PAIRS + strip + 1))
            north[at, :] = own_ref[strip, RIM:ROWS, :]
            south[at, :] = own_ref[strip, 0:RIM, :]

    pl.when(even_lat)(lambda: rows_out(True))
    pl.when(jnp.logical_not(even_lat))(lambda: rows_out(False))


def layer(thick, zonal, merid, slope_x, slope_y, depth, turn):
    (h, hE, hW, hN, hS), (u, uE, uW, uN, uS), (v, vE, vW, vN, vS) = thick, zonal, merid
    half = 0.5 * time_step
    flux = ((depth + hE) * uE - (depth + hW) * uW) + ((depth + hN) * vN - (depth + hS) * vS)
    h_new = 0.25 * ((hE + hW) + (hN + hS)) - half * flux
    u_new = 0.25 * ((uE + uW) + (uN + uS)) - (
        half * (u * (uE - uW) + v * (uN - uS) + slope_x) - turn * v
    )
    v_new = 0.25 * ((vE + vW) + (vN + vS)) - (
        half * (u * (vE - vW) + v * (vN - vS) + slope_y) + turn * u
    )
    return h_new, u_new, v_new


def advance(stencil, turn):
    top, low = stencil[0], stencil[3]
    top_x, top_y = top[1] - top[2], top[3] - top[4]
    low_x, low_y = low[1] - low[2], low[3] - low[4]
    sum_x, sum_y = top_x + low_x, top_y + low_y
    upper = layer(top, stencil[1], stencil[2], sum_x, sum_y, depth_top, turn)
    lower = layer(low, stencil[4], stencil[5], sum_x + 0.5 * low_x, sum_y + 0.5 * low_y, depth_low, turn)
    return upper + lower


def split(value):
    high = value.astype(jnp.bfloat16)
    rest = value - high.astype(f32)
    middle = rest.astype(jnp.bfloat16)
    return high, middle, (rest - middle.astype(f32)).astype(jnp.bfloat16)


def sweep(read, emit, read_strip, emit_strip, inner, turn):
    lane = iota((ROWS, COLS), 1)

    def members_step(members, which, shifts):
        stencils = []
        for member, shift in zip(members, shifts):
            stencil = []
            for field in range(FIELDS):
                c, n, s = read(member * FIELDS + field)
                beyond = read_strip(which, field)[0]
                if shift is not None:
                    beyond = pltpu.roll(beyond, COLS - shift, 1)
                e = pltpu.roll(jnp.where(lane == 0, beyond, c), COLS - 1, 1)
                w = pltpu.roll(jnp.where(lane == COLS - 1, beyond, c), 1, 1)
                stencil.append((c, e, w, n, s))
            stencils.append(stencil)
        if emit_strip is not None:
            for field in range(FIELDS):
                if shifts[0] is None:
                    inner[which, field] = stencils[0][field][0]
                    continue
                total = inner[which, field]
                for shift, stencil in zip(shifts, stencils):
                    edge = ((lane - shift + 1) & (COLS - 1)) < 2
                    total = jnp.where(edge, pltpu.roll(stencil[field][0], shift, 1), total)
                inner[which, field] = total
        for member, stencil in zip(members, stencils):
            for field, value in enumerate(advance(stencil, turn)):
                emit(member * FIELDS + field, value)

    def group_step(index, carry):
        members = [GROUP * index + k for k in range(GROUP)]
        members_step(members, 0, [8 * member for member in members])
        return carry

    lax.fori_loop(0, DIRS // GROUP, group_step, 0)
    members_step([DIRS], 1, [None])
    if emit_strip is None:
        return
    for which in range(2):
        stencil = []
        for field in range(FIELDS):
            c, n, s = read_strip(which, field)
            beyond = inner[which, field]
            e = pltpu.roll(jnp.where((lane & 7) == 0, beyond, c), COLS - 1, 1)
            w = pltpu.roll(jnp.where((lane & 7) == 7, beyond, c), 1, 1)
            stencil.append((c, e, w, n, s))
        for field, value in enumerate(advance(stencil, turn)):
            emit_strip(which, field, value)


def row_terms(first, second):
    lats = lax.axis_size("lat")
    sub = iota((ROWS, COLS), 0)
    row = jnp.where(sub < RIM, sub + first, sub - RIM + second) + lax.axis_index("lat") * ROWS
    inside = (row >= 0) & (row < lats * ROWS)
    turn = time_step * (0.5 * (2.0 * (row.astype(f32) + 0.5) / float(lats * ROWS) - 1.0))
    return inside, turn


def spread_strips(blocks, strips, first, last, at):
    for strip in range(STRIPS):
        for field in range(FIELDS) if strip == FIELDS else [strip]:
            block = blocks(strip)
            if strip == FIELDS and field:
                block = pltpu.roll(block, COLS - 8 * field, 1)
            strips[strip // FIELDS, field, at : at + last - first, :] = block[first:last, :]


def interior_kernel(x_ref, own_ref, *refs):
    levels, strip_levels, inner = [x_ref, *refs[0:3]], refs[3:7], refs[7]
    _, turn = row_terms(0, RIM)
    spread_strips(lambda strip: own_ref[strip], strip_levels[0], 0, ROWS, HOME)
    for step in range(SUBSTEPS - 1):
        old, fresh = levels[step], levels[step + 1]
        old_strips, fresh_strips = strip_levels[step], strip_levels[step + 1]

        def read(pair, old=old):
            return [old[pair, HOME + d : HOME + d + ROWS, :] for d in (0, 1, -1)]

        def emit(pair, value, fresh=fresh):
            fresh[pair, HOME : HOME + ROWS, :] = value

        def read_strip(which, field, old_strips=old_strips):
            return [old_strips[which, field, HOME + d : HOME + d + ROWS, :] for d in (0, 1, -1)]

        def emit_strip(which, field, value, fresh_strips=fresh_strips):
            fresh_strips[which, field, HOME : HOME + ROWS, :] = value

        sweep(read, emit, read_strip, emit_strip, inner, turn)


def forecast_kernel(*refs):
    first_ref, second_ref, count_ref, index_hbm, value_hbm, weight_hbm = refs[8:14]
    states, strips = refs[14:18], refs[18:22]
    modes_ref, mean_ref, pay_ref, inner, final, seen, gram, index_ref, value_ref, weight_ref, sems = refs[22:]
    moves = [
        pltpu.make_async_copy(source, target, sems.at[place])
        for place, (source, target) in enumerate(
            [(index_hbm, index_ref), (value_hbm, value_ref), (weight_hbm, weight_ref)]
        )
    ]
    for move in moves:
        move.start()
    lats = lax.axis_size("lat")
    even = (lax.axis_index("lat") & 1) == 0

    def rows_in(north_first):
        north, south = (first_ref, second_ref) if north_first else (second_ref, first_ref)
        for pair in range(PAIRS):
            at = slice(RIM * pair, RIM * (pair + 1))
            states[0][pair, HOME - RIM : HOME, :] = south[at, :]
            states[0][pair, HOME + ROWS : HOME + ROWS + RIM, :] = north[at, :]

        def corner(rows):
            return lambda strip: rows[RIM * (PAIRS + strip) : RIM * (PAIRS + strip + 1), :]

        spread_strips(corner(south), strips[0], 0, RIM, HOME - RIM)
        spread_strips(corner(north), strips[0], 0, RIM, HOME + ROWS)

    pl.when(even)(lambda: rows_in(True))
    pl.when(jnp.logical_not(even))(lambda: rows_in(False))
    upper = iota((ROWS, COLS), 0) < RIM
    for step in range(SUBSTEPS - 1):
        low, high = step - 3, 7 - step
        inside, turn = row_terms(low, high)

        def both(ref, *at, low=low, high=high):
            return [
                jnp.where(
                    upper,
                    ref[(*at, slice(HOME + low + d, HOME + low + d + ROWS), slice(None))],
                    ref[(*at, slice(HOME + high - RIM + d, HOME + high + RIM + d), slice(None))],
                )
                for d in (0, 1, -1)
            ]

        def put(ref, value, *at, low=low, high=high, inside=inside):
            value = jnp.where(inside, value, 0.0)
            ref[(*at, slice(HOME + low, HOME + low + RIM), slice(None))] = value[0:RIM, :]
            ref[(*at, slice(HOME + high, HOME + high + RIM), slice(None))] = value[RIM:ROWS, :]

        sweep(
            lambda pair, step=step, both=both: both(states[step], pair),
            lambda pair, value, step=step, put=put: put(states[step + 1], value, pair),
            lambda which, field, step=step, both=both: both(strips[step], which, field),
            lambda which, field, value, step=step, put=put: put(strips[step + 1], value, which, field),
            inner,
            turn,
        )

    def own_rows(ref, *at):
        return [ref[(*at, slice(HOME + d, HOME + d + ROWS), slice(None))] for d in (0, 1, -1)]

    def finish(pair, value):
        final[pl.ds(pl.multiple_of(pair * ROWS, ROWS), ROWS), :] = value

    sweep(
        lambda pair: own_rows(states[3], pair),
        finish,
        lambda which, field: own_rows(strips[3], which, field),
        None,
        inner,
        row_terms(0, RIM)[1],
    )

    sub8 = iota((ROWS, COLS), 0)
    for move in moves:
        move.wait()
    cell = index_ref[...]
    column = jnp.broadcast_to(cell & (COLS - 1), (ROWS, COLS))
    at_row = jnp.broadcast_to(lax.shift_right_logical(cell, 7), (ROWS, COLS)) == sub8
    def block(member, field):
        at = (member * FIELDS + field) * ROWS
        return final[at : at + ROWS, :]

    for member in range(MEMBERS):
        surface = block(member, 0) + block(member, 3)
        picked = jnp.take_along_axis(surface, column, axis=1)
        seen[member : member + 1, :] = jnp.sum(jnp.where(at_row, picked, 0.0), axis=0, keepdims=True)

    for field in range(FIELDS):
        total = block(0, field)
        for member in range(1, MEMBERS):
            total = total + block(member, field)
        mean_ref[ROWS * field : ROWS * (field + 1), :] = total * (1.0 / MEMBERS)
    for tile in range(TILES):
        span = slice(COLS * tile, COLS * (tile + 1))
        parts = split(final[pl.ds(tile, DIRS, stride=TILES), :] - mean_ref[tile : tile + 1, :])
        for place, part in enumerate(parts):
            modes_ref[DIRS * place : DIRS * (place + 1), span] = part

    stack = modes_ref[...]
    blocks = lax.dot_general(stack, stack, (((1,), (1,)), ((), ())), preferred_element_type=f32)
    rows3 = blocks[0:DIRS, :] + (blocks[DIRS : 2 * DIRS, :] + blocks[2 * DIRS :, :])
    mode_gram = rows3[:, 0:DIRS] + (rows3[:, DIRS : 2 * DIRS] + rows3[:, 2 * DIRS :])

    observed = seen[...]
    obs_mean = jnp.sum(observed, axis=0, keepdims=True) * (1.0 / MEMBERS)
    anomaly = observed[0:DIRS, :] - obs_mean
    innovation = value_ref[...] - obs_mean
    live = (iota((1, COLS), 1) < count_ref[...]).astype(f32)
    weighted = anomaly * (weight_ref[...] * live / float(COLS * lats * lax.axis_size("lon")))
    obs_gram = lax.dot_general(
        weighted, anomaly, (((1,), (1,)), ((), ())), precision=highest, preferred_element_type=f32
    )
    obs_proj = jnp.sum(weighted * innovation, axis=1, keepdims=True)
    row, col = iota((DIRS, DIRS), 0), iota((DIRS, DIRS), 1)
    gram[...] = jnp.zeros((DIRS, COLS), f32)
    gram[:, 0:DIRS] = jnp.where(row < col, obs_gram, mode_gram)
    gram[:, DIRS : DIRS + 1] = jnp.sum(jnp.where(row == col, obs_gram, 0.0), axis=1, keepdims=True)
    gram[:, DIRS + 1 : DIRS + 2] = obs_proj
    packed = gram[0:4, :]
    for quarter in range(1, 4):
        packed = packed + pltpu.roll(gram[4 * quarter : 4 * quarter + 4, :], 32 * quarter, 1)
    pay_ref[...] = packed


def analysis_kernel(parts_ref, modes_ref, mean_ref, out_ref, spread_ref, gram):
    packed = jnp.sum(parts_ref[...], axis=0)
    for quarter in range(4):
        gram[4 * quarter : 4 * quarter + 4, :] = (
            pltpu.roll(packed, COLS - 32 * quarter, 1) if quarter else packed
        )
    joined = gram[...]
    row, col = iota((DIRS, DIRS), 0), iota((DIRS, DIRS), 1)
    square = joined[:, 0:DIRS]
    upper = jnp.where(row < col, square, 0.0)
    lower = jnp.where(row > col, square, 0.0)
    mode_gram = jnp.where(row == col, square, 0.0) + (lower + lower.T)
    obs_gram = jnp.where(row == col, joined[:, DIRS : DIRS + 1], 0.0) + (upper + upper.T)
    precision = obs_gram + (DIRS / forget) * (jnp.where(row == col, 1.0, 0.0) - 1.0 / MEMBERS)
    sub, lane = iota((DIRS, COLS), 0), iota((DIRS, COLS), 1)
    copies = 6 * DIRS
    gram[:, copies : copies + DIRS] = precision
    gram[:, copies + DIRS : copies + DIRS + 1] = joined[:, DIRS + 1 : DIRS + 2]
    unit = jnp.where((lane & (DIRS - 1)) == sub, 1.0, 0.0)
    work = jnp.where(lane < copies, unit, gram[...])
    work = jnp.where(lane <= copies + DIRS, work, 0.0)
    for first in range(0, DIRS, 16):
        pivots = range(first, first + 16)
        columns = [jnp.broadcast_to(work[:, copies + p : copies + p + 1], (DIRS, COLS)) for p in pivots]
        rows = []
        for k, pivot in enumerate(pivots):
            column, pivot_row = columns[k], work[pivot : pivot + 1, :]
            for q in range(k):
                factor = columns[q][pivot : pivot + 1, :]
                column = column - columns[q] * factor
                pivot_row = pivot_row - factor * rows[q]
            value = column[pivot : pivot + 1, :]
            inverse = lax.rsqrt(value)
            inverse = inverse * (1.5 - 0.5 * value * inverse * inverse)
            columns[k] = column * inverse
            rows.append(pivot_row * inverse)
        below = work
        for k in range(16):
            below = below - columns[k] * rows[k]
        work = jnp.where(sub >= first + 16, below, work)
        for k, pivot in enumerate(pivots):
            work = jnp.where(sub == pivot, rows[k], work)
    inverse_factor = work[:, :copies]
    solved = work[:, copies + DIRS : copies + DIRS + 1]
    weights = jnp.sum(solved * inverse_factor, axis=0, keepdims=True)
    spare = (math.sqrt(MEMBERS) - 1.0) / DIRS
    scale = math.sqrt(DIRS)
    sums = jnp.sum(inverse_factor, axis=0, keepdims=True)
    rotation_t = jnp.concatenate(
        [
            scale * inverse_factor + (scale * (spare - 1.0) / MEMBERS) * sums,
            (-scale * (1.0 + DIRS * spare) / MEMBERS) * sums,
        ],
        axis=0,
    )
    coefficient_t = rotation_t + weights
    high, middle, low = split(coefficient_t)
    place = iota((MEMBERS, copies), 1)
    stack = jnp.where(place < 3 * DIRS, high.astype(f32), jnp.where(place < 5 * DIRS, middle.astype(f32), low.astype(f32)))
    stack = stack.astype(jnp.bfloat16)
    for field in range(FIELDS):
        span = slice(field * ROWS * COLS, (field + 1) * ROWS * COLS)
        parts = jnp.concatenate(
            [modes_ref[:, span], modes_ref[0 : 2 * DIRS, span], modes_ref[0:DIRS, span]], axis=0
        )
        update = jnp.dot(stack, parts, preferred_element_type=f32)
        for row_here in range(ROWS):
            tile = field * ROWS + row_here
            out_ref[pl.ds(tile, MEMBERS, stride=TILES), :] = (
                update[:, COLS * row_here : COLS * (row_here + 1)] + mean_ref[tile : tile + 1, :]
            )
    rotation_t = rotation_t[:, 0:DIRS]
    half_way = jnp.dot(rotation_t, mode_gram, precision=highest, preferred_element_type=f32)
    spread = lax.dot_general(
        half_way, rotation_t, (((1,), (1,)), ((), ())), precision=highest, preferred_element_type=f32
    )
    spread_ref[...] = spread / float(CELLS * lax.axis_size("lat") * lax.axis_size("lon"))


def neighbours(axis, parity, wrap):
    count = lax.axis_size(axis)
    pairs = [(i, i + 1) for i in range(parity, count - 1, 2)]
    if wrap and parity:
        pairs.append((count - 1, 0))
    return pairs + [(j, i) for i, j in pairs]


def all_parts(part, groups):
    count = len(groups[0])
    return lax.all_to_all(
        jnp.broadcast_to(part[None], (count,) + part.shape), ("lon", "lat"), 0, 0, axis_index_groups=groups
    )


def on_device(sample_collection, obs_index, obs_count, obs_value, obs_weight):
    lat_tiles, lon_tiles = lax.axis_size("lat"), lax.axis_size("lon")
    small = pltpu.CompilerParams(vmem_limit_bytes=20 * 2**20)
    in_hbm = pl.BlockSpec(memory_space=pltpu.HBM)
    blocks, index, value, weight = [
        pltpu.with_memory_space_constraint(array, pltpu.HBM)
        for array in (
            sample_collection.reshape(PAIRS, ROWS, COLS),
            obs_index.reshape(1, COLS),
            obs_value.reshape(1, COLS),
            obs_weight.reshape(1, COLS),
        )
    ]
    strips_shape = jax.ShapeDtypeStruct((STRIPS, ROWS, COLS), f32)
    level_shape = jax.ShapeDtypeStruct((PAIRS, DEEP, COLS), f32)
    strip_level = jax.ShapeDtypeStruct((2, FIELDS, DEEP, COLS), f32)
    strip_msg, here = pl.pallas_call(
        pack_kernel,
        out_shape=[strips_shape, level_shape],
        in_specs=[in_hbm],
        out_specs=vmem(2),
        scratch_shapes=[pltpu.SemaphoreType.DMA],
        compiler_params=small,
    )(blocks)
    strip1 = lax.ppermute(strip_msg, "lon", neighbours("lon", 0, True))
    strip2 = lax.ppermute(strip_msg, "lon", neighbours("lon", 1, True))
    own_strip, first_msg, second_msg = pl.pallas_call(
        message_kernel,
        out_shape=[strips_shape] + [jax.ShapeDtypeStruct((MSG_ROWS, COLS), f32)] * 2,
        in_specs=vmem(3),
        out_specs=vmem(3),
        compiler_params=small,
    )(here, strip1, strip2)
    first = lax.ppermute(first_msg, "lat", neighbours("lat", 0, False))
    second = lax.ppermute(second_msg, "lat", neighbours("lat", 1, False))
    interior = pl.pallas_call(
        interior_kernel,
        out_shape=[level_shape] * 3 + [strip_level] * 4,
        in_specs=vmem(2),
        out_specs=vmem(7),
        scratch_shapes=[pltpu.VMEM((2, FIELDS, ROWS, COLS), f32)],
        compiler_params=small,
        cost_estimate=pl.CostEstimate(flops=40_000_000, bytes_accessed=2_000_000, transcendentals=0),
    )(here, own_strip)

    *_, modes, mean, part = pl.pallas_call(
        forecast_kernel,
        out_shape=[level_shape] * 4
        + [strip_level] * 4
        + [
            jax.ShapeDtypeStruct((3 * DIRS, CELLS), jnp.bfloat16),
            jax.ShapeDtypeStruct((TILES, COLS), f32),
            jax.ShapeDtypeStruct((4, COLS), f32),
        ],
        in_specs=vmem(11) + [in_hbm] * 3,
        out_specs=vmem(11),
        scratch_shapes=[
            pltpu.VMEM((2, FIELDS, ROWS, COLS), f32),
            pltpu.VMEM((PAIRS * ROWS, COLS), f32),
            pltpu.VMEM((MEMBERS, COLS), f32),
            pltpu.VMEM((DIRS, COLS), f32),
            pltpu.VMEM((1, COLS), jnp.int32),
            pltpu.VMEM((1, COLS), f32),
            pltpu.VMEM((1, COLS), f32),
            pltpu.SemaphoreType.DMA((3,)),
        ],
        input_output_aliases={level: level for level in range(8)},
        compiler_params=small,
    )(here, *interior, first, second, jnp.broadcast_to(obs_count, (1, COLS)), index, value, weight)

    fine = min(16, lon_tiles)
    index = [[lon * lat_tiles + lat for lat in range(lat_tiles)] for lon in range(lon_tiles)]
    near = [
        [index[base + k][lat] for k in range(fine)] for base in range(0, lon_tiles, fine) for lat in range(lat_tiles)
    ]
    far = [[index[lon][lat] for lon in range(k, lon_tiles, fine) for lat in range(lat_tiles)] for k in range(fine)]
    part = jnp.sum(all_parts(part, near), axis=0)
    parts = all_parts(part, far)
    analysis, spread = pl.pallas_call(
        analysis_kernel,
        out_shape=[jax.ShapeDtypeStruct((PAIRS * ROWS, COLS), f32), jax.ShapeDtypeStruct((MEMBERS, MEMBERS), f32)],
        in_specs=vmem(3),
        out_specs=vmem(2),
        scratch_shapes=[pltpu.VMEM((DIRS, COLS), f32)],
        compiler_params=small,
    )(parts, modes, mean)
    return analysis.reshape(sample_collection.shape), spread


def solution(mesh):
    return jax.shard_map(
        on_device,
        mesh=mesh,
        in_specs=(
            P(None, None, "lat", "lon"),
            P("lat", "lon", None),
            P("lat", "lon"),
            P("lat", "lon", None),
            P("lat", "lon", None),
        ),
        out_specs=(P(None, None, "lat", "lon"), P()),
        check_vma=False,
    )
```

```python
import math

import jax
import jax.numpy as jnp
from jax import lax
from jax.experimental import pallas as pl
from jax.experimental.pallas import tpu as pltpu
from jax.sharding import PartitionSpec as P


DIRS = 16
MEMBERS = 17
FIELDS = 6
PAIRS = MEMBERS * FIELDS
SUBSTEPS = 4
RIM = 4
ROWS = 8
COLS = 128
CELLS = FIELDS * ROWS * COLS
TILES = FIELDS * ROWS
HOME = 12
DEEP = 32
GROUP = 2
STRIPS = FIELDS + 1
MSG_ROWS = (PAIRS + STRIPS) * RIM

time_step = 0.15
depth_top = 4.0
depth_low = 6.0
forget = 0.9
highest = lax.Precision.HIGHEST
f32 = jnp.float32


def iota(shape, axis):
    return lax.broadcasted_iota(jnp.int32, shape, axis)


def vmem(count):
    return [pl.BlockSpec(memory_space=pltpu.VMEM)] * count


def pack_kernel(x_hbm, strip_ref, x_ref, sem):
    move = pltpu.make_async_copy(x_hbm, x_ref.at[:, HOME : HOME + ROWS, :], sem)
    move.start()
    move.wait()
    lane = iota((ROWS, COLS), 1)
    for strip in range(STRIPS):
        total = jnp.zeros((ROWS, COLS), f32)
        for place in range(DIRS if strip < FIELDS else FIELDS):
            pair = place * FIELDS + strip if strip < FIELDS else DIRS * FIELDS + place
            block = x_ref[pair, HOME : HOME + ROWS, :]
            moved = pltpu.roll(block, 8 * place, 1) if place else block
            mask = ((lane - (8 * place - 4)) & (COLS - 1)) < 8
            total = jnp.where(mask, moved, total)
        strip_ref[strip] = total


def message_kernel(x_ref, strip1_ref, strip2_ref, own_ref, first_ref, second_ref):
    even_lon = (lax.axis_index("lon") & 1) == 0
    even_lat = (lax.axis_index("lat") & 1) == 0
    eastern = (iota((ROWS, COLS), 1) & 7) < RIM

    def merge(first_is_east):
        east, west = (strip1_ref, strip2_ref) if first_is_east else (strip2_ref, strip1_ref)
        for strip in range(STRIPS):
            own_ref[strip] = jnp.where(eastern, east[strip], west[strip])

    pl.when(even_lon)(lambda: merge(True))
    pl.when(jnp.logical_not(even_lon))(lambda: merge(False))

    def rows_out(north_first):
        north, south = (first_ref, second_ref) if north_first else (second_ref, first_ref)
        for pair in range(PAIRS):
            at = slice(RIM * pair, RIM * (pair + 1))
            north[at, :] = x_ref[pair, HOME + RIM : HOME + ROWS, :]
            south[at, :] = x_ref[pair, HOME : HOME + RIM, :]
        for strip in range(STRIPS):
            at = slice(RIM * (PAIRS + strip), RIM * (PAIRS + strip + 1))
            north[at, :] = own_ref[strip, RIM:ROWS, :]
            south[at, :] = own_ref[strip, 0:RIM, :]

    pl.when(even_lat)(lambda: rows_out(True))
    pl.when(jnp.logical_not(even_lat))(lambda: rows_out(False))


def layer(thick, zonal, merid, slope_x, slope_y, depth, turn):
    (h, hE, hW, hN, hS), (u, uE, uW, uN, uS), (v, vE, vW, vN, vS) = thick, zonal, merid
    half = 0.5 * time_step
    flux = ((depth + hE) * uE - (depth + hW) * uW) + ((depth + hN) * vN - (depth + hS) * vS)
    h_new = 0.25 * ((hE + hW) + (hN + hS)) - half * flux
    u_new = 0.25 * ((uE + uW) + (uN + uS)) - (
        half * (u * (uE - uW) + v * (uN - uS) + slope_x) - turn * v
    )
    v_new = 0.25 * ((vE + vW) + (vN + vS)) - (
        half * (u * (vE - vW) + v * (vN - vS) + slope_y) + turn * u
    )
    return h_new, u_new, v_new


def advance(stencil, turn):
    top, low = stencil[0], stencil[3]
    top_x, top_y = top[1] - top[2], top[3] - top[4]
    low_x, low_y = low[1] - low[2], low[3] - low[4]
    sum_x, sum_y = top_x + low_x, top_y + low_y
    upper = layer(top, stencil[1], stencil[2], sum_x, sum_y, depth_top, turn)
    lower = layer(low, stencil[4], stencil[5], sum_x + 0.5 * low_x, sum_y + 0.5 * low_y, depth_low, turn)
    return upper + lower


def split(value):
    high = value.astype(jnp.bfloat16)
    rest = value - high.astype(f32)
    middle = rest.astype(jnp.bfloat16)
    return high, middle, (rest - middle.astype(f32)).astype(jnp.bfloat16)


def sweep(read, emit, read_strip, emit_strip, inner, turn):
    lane = iota((ROWS, COLS), 1)

    def members_step(members, which, shifts):
        stencils = []
        for member, shift in zip(members, shifts):
            stencil = []
            for field in range(FIELDS):
                c, n, s = read(member * FIELDS + field)
                beyond = read_strip(which, field)[0]
                if shift is not None:
                    beyond = pltpu.roll(beyond, COLS - shift, 1)
                e = pltpu.roll(jnp.where(lane == 0, beyond, c), COLS - 1, 1)
                w = pltpu.roll(jnp.where(lane == COLS - 1, beyond, c), 1, 1)
                stencil.append((c, e, w, n, s))
            stencils.append(stencil)
        if emit_strip is not None:
            for field in range(FIELDS):
                if shifts[0] is None:
                    inner[which, field] = stencils[0][field][0]
                    continue
                total = inner[which, field]
                for shift, stencil in zip(shifts, stencils):
                    edge = ((lane - shift + 1) & (COLS - 1)) < 2
                    total = jnp.where(edge, pltpu.roll(stencil[field][0], shift, 1), total)
                inner[which, field] = total
        for member, stencil in zip(members, stencils):
            for field, value in enumerate(advance(stencil, turn)):
                emit(member * FIELDS + field, value)

    def group_step(index, carry):
        for part in range(2):
            members = [GROUP * (2 * index + part) + k for k in range(GROUP)]
            members_step(members, 0, [8 * member for member in members])
        return carry

    lax.fori_loop(0, DIRS // GROUP // 2, group_step, 0)
    members_step([DIRS], 1, [None])
    if emit_strip is None:
        return
    for which in range(2):
        stencil = []
        for field in range(FIELDS):
            c, n, s = read_strip(which, field)
            beyond = inner[which, field]
            e = pltpu.roll(jnp.where((lane & 7) == 0, beyond, c), COLS - 1, 1)
            w = pltpu.roll(jnp.where((lane & 7) == 7, beyond, c), 1, 1)
            stencil.append((c, e, w, n, s))
        for field, value in enumerate(advance(stencil, turn)):
            emit_strip(which, field, value)


def row_terms(first, second):
    lats = lax.axis_size("lat")
    sub = iota((ROWS, COLS), 0)
    row = jnp.where(sub < RIM, sub + first, sub - RIM + second) + lax.axis_index("lat") * ROWS
    inside = (row >= 0) & (row < lats * ROWS)
    turn = time_step * (0.5 * (2.0 * (row.astype(f32) + 0.5) / float(lats * ROWS) - 1.0))
    return inside, turn


def spread_strips(blocks, strips, first, last, at):
    for strip in range(STRIPS):
        for field in range(FIELDS) if strip == FIELDS else [strip]:
            block = blocks(strip)
            if strip == FIELDS and field:
                block = pltpu.roll(block, COLS - 8 * field, 1)
            strips[strip // FIELDS, field, at : at + last - first, :] = block[first:last, :]


def interior_kernel(x_ref, own_ref, *refs):
    levels, strip_levels, inner = [x_ref, *refs[0:3]], refs[3:7], refs[7]
    _, turn = row_terms(0, RIM)
    spread_strips(lambda strip: own_ref[strip], strip_levels[0], 0, ROWS, HOME)
    for step in range(SUBSTEPS - 1):
        old, fresh = levels[step], levels[step + 1]
        old_strips, fresh_strips = strip_levels[step], strip_levels[step + 1]

        def read(pair, old=old):
            return [old[pair, HOME + d : HOME + d + ROWS, :] for d in (0, 1, -1)]

        def emit(pair, value, fresh=fresh):
            fresh[pair, HOME : HOME + ROWS, :] = value

        def read_strip(which, field, old_strips=old_strips):
            return [old_strips[which, field, HOME + d : HOME + d + ROWS, :] for d in (0, 1, -1)]

        def emit_strip(which, field, value, fresh_strips=fresh_strips):
            fresh_strips[which, field, HOME : HOME + ROWS, :] = value

        sweep(read, emit, read_strip, emit_strip, inner, turn)


def forecast_kernel(*refs):
    levels, strip_levels = refs[0:4], refs[4:8]
    first_ref, second_ref, count_ref, index_hbm, value_hbm, weight_hbm = refs[8:14]
    modes_ref, mean_ref, pay_ref, inner, final, seen, gram, index_ref, value_ref, weight_ref, sems = refs[14:25]
    states, strips = refs[25:29], refs[29:33]
    moves = [
        pltpu.make_async_copy(source, target, sems.at[place])
        for place, (source, target) in enumerate(
            [(index_hbm, index_ref), (value_hbm, value_ref), (weight_hbm, weight_ref)]
        )
    ]
    for move in moves:
        move.start()
    lats = lax.axis_size("lat")
    even = (lax.axis_index("lat") & 1) == 0

    def rows_in(north_first):
        north, south = (first_ref, second_ref) if north_first else (second_ref, first_ref)
        for pair in range(PAIRS):
            at = slice(RIM * pair, RIM * (pair + 1))
            states[0][pair, HOME - RIM : HOME, :] = south[at, :]
            states[0][pair, HOME + ROWS : HOME + ROWS + RIM, :] = north[at, :]

        def corner(rows):
            return lambda strip: rows[RIM * (PAIRS + strip) : RIM * (PAIRS + strip + 1), :]

        spread_strips(corner(south), strips[0], 0, RIM, HOME - RIM)
        spread_strips(corner(north), strips[0], 0, RIM, HOME + ROWS)

    pl.when(even)(lambda: rows_in(True))
    pl.when(jnp.logical_not(even))(lambda: rows_in(False))
    home = slice(HOME, HOME + ROWS)
    for source, target in zip(levels, states):
        for pair in range(PAIRS):
            target[pair, home, :] = source[pair, home, :]
    for source, target in zip(strip_levels, strips):
        for which in range(2):
            for field in range(FIELDS):
                target[which, field, home, :] = source[which, field, home, :]

    upper = iota((ROWS, COLS), 0) < RIM
    for step in range(SUBSTEPS - 1):
        low, high = step - 3, 7 - step
        inside, turn = row_terms(low, high)

        def both(ref, *at, low=low, high=high):
            return [
                jnp.where(
                    upper,
                    ref[(*at, slice(HOME + low + d, HOME + low + d + ROWS), slice(None))],
                    ref[(*at, slice(HOME + high - RIM + d, HOME + high + RIM + d), slice(None))],
                )
                for d in (0, 1, -1)
            ]

        def put(ref, value, *at, low=low, high=high, inside=inside):
            value = jnp.where(inside, value, 0.0)
            ref[(*at, slice(HOME + low, HOME + low + RIM), slice(None))] = value[0:RIM, :]
            ref[(*at, slice(HOME + high, HOME + high + RIM), slice(None))] = value[RIM:ROWS, :]

        sweep(
            lambda pair, step=step, both=both: both(states[step], pair),
            lambda pair, value, step=step, put=put: put(states[step + 1], value, pair),
            lambda which, field, step=step, both=both: both(strips[step], which, field),
            lambda which, field, value, step=step, put=put: put(strips[step + 1], value, which, field),
            inner,
            turn,
        )

    def own_rows(ref, *at):
        return [ref[(*at, slice(HOME + d, HOME + d + ROWS), slice(None))] for d in (0, 1, -1)]

    def finish(pair, value):
        final[pl.ds(pl.multiple_of(pair * ROWS, ROWS), ROWS), :] = value

    sweep(
        lambda pair: own_rows(states[3], pair),
        finish,
        lambda which, field: own_rows(strips[3], which, field),
        None,
        inner,
        row_terms(0, RIM)[1],
    )

    sub8 = iota((ROWS, COLS), 0)
    for move in moves:
        move.wait()
    cell = index_ref[...]
    column = jnp.broadcast_to(cell & (COLS - 1), (ROWS, COLS))
    at_row = jnp.broadcast_to(lax.shift_right_logical(cell, 7), (ROWS, COLS)) == sub8
    def block(member, field):
        at = (member * FIELDS + field) * ROWS
        return final[at : at + ROWS, :]

    for member in range(MEMBERS):
        surface = block(member, 0) + block(member, 3)
        picked = jnp.take_along_axis(surface, column, axis=1)
        seen[member : member + 1, :] = jnp.sum(jnp.where(at_row, picked, 0.0), axis=0, keepdims=True)

    for field in range(FIELDS):
        total = block(0, field)
        for member in range(1, MEMBERS):
            total = total + block(member, field)
        mean_ref[ROWS * field : ROWS * (field + 1), :] = total * (1.0 / MEMBERS)
    for tile in range(TILES):
        span = slice(COLS * tile, COLS * (tile + 1))
        parts = split(final[pl.ds(tile, DIRS, stride=TILES), :] - mean_ref[tile : tile + 1, :])
        for place, part in enumerate(parts):
            modes_ref[DIRS * place : DIRS * (place + 1), span] = part

    stack = modes_ref[...]
    blocks = lax.dot_general(stack, stack, (((1,), (1,)), ((), ())), preferred_element_type=f32)
    rows3 = blocks[0:DIRS, :] + (blocks[DIRS : 2 * DIRS, :] + blocks[2 * DIRS :, :])
    mode_gram = rows3[:, 0:DIRS] + (rows3[:, DIRS : 2 * DIRS] + rows3[:, 2 * DIRS :])

    observed = seen[...]
    obs_mean = jnp.sum(observed, axis=0, keepdims=True) * (1.0 / MEMBERS)
    anomaly = observed[0:DIRS, :] - obs_mean
    innovation = value_ref[...] - obs_mean
    live = (iota((1, COLS), 1) < count_ref[...]).astype(f32)
    weighted = anomaly * (weight_ref[...] * live / float(COLS * lats * lax.axis_size("lon")))
    obs_gram = lax.dot_general(
        weighted, anomaly, (((1,), (1,)), ((), ())), precision=highest, preferred_element_type=f32
    )
    obs_proj = jnp.sum(weighted * innovation, axis=1, keepdims=True)
    row, col = iota((DIRS, DIRS), 0), iota((DIRS, DIRS), 1)
    gram[...] = jnp.zeros((DIRS, COLS), f32)
    gram[:, 0:DIRS] = jnp.where(row < col, obs_gram, mode_gram)
    gram[:, DIRS : DIRS + 1] = jnp.sum(jnp.where(row == col, obs_gram, 0.0), axis=1, keepdims=True)
    gram[:, DIRS + 1 : DIRS + 2] = obs_proj
    packed = gram[0:4, :]
    for quarter in range(1, 4):
        packed = packed + pltpu.roll(gram[4 * quarter : 4 * quarter + 4, :], 32 * quarter, 1)
    pay_ref[...] = packed


def analysis_kernel(parts_ref, modes_ref, mean_ref, out_ref, spread_ref, gram):
    packed = jnp.sum(parts_ref[...], axis=0)
    for quarter in range(4):
        gram[4 * quarter : 4 * quarter + 4, :] = (
            pltpu.roll(packed, COLS - 32 * quarter, 1) if quarter else packed
        )
    joined = gram[...]
    row, col = iota((DIRS, DIRS), 0), iota((DIRS, DIRS), 1)
    square = joined[:, 0:DIRS]
    upper = jnp.where(row < col, square, 0.0)
    lower = jnp.where(row > col, square, 0.0)
    mode_gram = jnp.where(row == col, square, 0.0) + (lower + lower.T)
    obs_gram = jnp.where(row == col, joined[:, DIRS : DIRS + 1], 0.0) + (upper + upper.T)
    precision = obs_gram + (DIRS / forget) * (jnp.where(row == col, 1.0, 0.0) - 1.0 / MEMBERS)
    sub, lane = iota((DIRS, COLS), 0), iota((DIRS, COLS), 1)
    copies = 6 * DIRS
    gram[:, copies : copies + DIRS] = precision
    gram[:, copies + DIRS : copies + DIRS + 1] = joined[:, DIRS + 1 : DIRS + 2]
    unit = jnp.where((lane & (DIRS - 1)) == sub, 1.0, 0.0)
    work = jnp.where(lane < copies, unit, gram[...])
    work = jnp.where(lane <= copies + DIRS, work, 0.0)
    for first in range(0, DIRS, 16):
        pivots = range(first, first + 16)
        columns = [jnp.broadcast_to(work[:, copies + p : copies + p + 1], (DIRS, COLS)) for p in pivots]
        rows = []
        for k, pivot in enumerate(pivots):
            column, pivot_row = columns[k], work[pivot : pivot + 1, :]
            for q in range(k):
                factor = columns[q][pivot : pivot + 1, :]
                column = column - columns[q] * factor
                pivot_row = pivot_row - factor * rows[q]
            value = column[pivot : pivot + 1, :]
            inverse = lax.rsqrt(value)
            inverse = inverse * (1.5 - 0.5 * value * inverse * inverse)
            columns[k] = column * inverse
            rows.append(pivot_row * inverse)
        below = work
        for k in range(16):
            below = below - columns[k] * rows[k]
        work = jnp.where(sub >= first + 16, below, work)
        for k, pivot in enumerate(pivots):
            work = jnp.where(sub == pivot, rows[k], work)
    inverse_factor = work[:, :copies]
    solved = work[:, copies + DIRS : copies + DIRS + 1]
    weights = jnp.sum(solved * inverse_factor, axis=0, keepdims=True)
    spare = (math.sqrt(MEMBERS) - 1.0) / DIRS
    scale = math.sqrt(DIRS)
    sums = jnp.sum(inverse_factor, axis=0, keepdims=True)
    rotation_t = jnp.concatenate(
        [
            scale * inverse_factor + (scale * (spare - 1.0) / MEMBERS) * sums,
            (-scale * (1.0 + DIRS * spare) / MEMBERS) * sums,
        ],
        axis=0,
    )
    coefficient_t = rotation_t + weights
    high, middle, low = split(coefficient_t)
    place = iota((MEMBERS, copies), 1)
    stack = jnp.where(place < 3 * DIRS, high.astype(f32), jnp.where(place < 5 * DIRS, middle.astype(f32), low.astype(f32)))
    stack = stack.astype(jnp.bfloat16)
    for field in range(FIELDS):
        span = slice(field * ROWS * COLS, (field + 1) * ROWS * COLS)
        parts = jnp.concatenate(
            [modes_ref[:, span], modes_ref[0 : 2 * DIRS, span], modes_ref[0:DIRS, span]], axis=0
        )
        update = jnp.dot(stack, parts, preferred_element_type=f32)
        for row_here in range(ROWS):
            tile = field * ROWS + row_here
            out_ref[pl.ds(tile, MEMBERS, stride=TILES), :] = (
                update[:, COLS * row_here : COLS * (row_here + 1)] + mean_ref[tile : tile + 1, :]
            )
    rotation_t = rotation_t[:, 0:DIRS]
    half_way = jnp.dot(rotation_t, mode_gram, precision=highest, preferred_element_type=f32)
    spread = lax.dot_general(
        half_way, rotation_t, (((1,), (1,)), ((), ())), precision=highest, preferred_element_type=f32
    )
    spread_ref[...] = spread / float(CELLS * lax.axis_size("lat") * lax.axis_size("lon"))


def neighbours(axis, parity, wrap):
    count = lax.axis_size(axis)
    pairs = [(i, i + 1) for i in range(parity, count - 1, 2)]
    if wrap and parity:
        pairs.append((count - 1, 0))
    return pairs + [(j, i) for i, j in pairs]


def all_parts(part, groups):
    count = len(groups[0])
    return lax.all_to_all(
        jnp.broadcast_to(part[None], (count,) + part.shape), ("lon", "lat"), 0, 0, axis_index_groups=groups
    )


def on_device(sample_collection, obs_index, obs_count, obs_value, obs_weight):
    lat_tiles, lon_tiles = lax.axis_size("lat"), lax.axis_size("lon")
    small = pltpu.CompilerParams(vmem_limit_bytes=20 * 2**20)
    in_hbm = pl.BlockSpec(memory_space=pltpu.HBM)
    blocks, index, value, weight = [
        pltpu.with_memory_space_constraint(array, pltpu.HBM)
        for array in (
            sample_collection.reshape(PAIRS, ROWS, COLS),
            obs_index.reshape(1, COLS),
            obs_value.reshape(1, COLS),
            obs_weight.reshape(1, COLS),
        )
    ]
    strips_shape = jax.ShapeDtypeStruct((STRIPS, ROWS, COLS), f32)
    level_shape = jax.ShapeDtypeStruct((PAIRS, DEEP, COLS), f32)
    strip_level = jax.ShapeDtypeStruct((2, FIELDS, DEEP, COLS), f32)
    strip_msg, here = pl.pallas_call(
        pack_kernel,
        out_shape=[strips_shape, level_shape],
        in_specs=[in_hbm],
        out_specs=vmem(2),
        scratch_shapes=[pltpu.SemaphoreType.DMA],
        compiler_params=small,
    )(blocks)
    strip1 = lax.ppermute(strip_msg, "lon", neighbours("lon", 0, True))
    strip2 = lax.ppermute(strip_msg, "lon", neighbours("lon", 1, True))
    own_strip, first_msg, second_msg = pl.pallas_call(
        message_kernel,
        out_shape=[strips_shape] + [jax.ShapeDtypeStruct((MSG_ROWS, COLS), f32)] * 2,
        in_specs=vmem(3),
        out_specs=vmem(3),
        compiler_params=small,
    )(here, strip1, strip2)
    first = lax.ppermute(first_msg, "lat", neighbours("lat", 0, False))
    second = lax.ppermute(second_msg, "lat", neighbours("lat", 1, False))
    interior = pl.pallas_call(
        interior_kernel,
        out_shape=[level_shape] * 3 + [strip_level] * 4,
        in_specs=vmem(2),
        out_specs=vmem(7),
        scratch_shapes=[pltpu.VMEM((2, FIELDS, ROWS, COLS), f32)],
        compiler_params=small,
        cost_estimate=pl.CostEstimate(flops=40_000_000, bytes_accessed=2_000_000, transcendentals=0),
    )(here, own_strip)

    modes, mean, part = pl.pallas_call(
        forecast_kernel,
        out_shape=[
            jax.ShapeDtypeStruct((3 * DIRS, CELLS), jnp.bfloat16),
            jax.ShapeDtypeStruct((TILES, COLS), f32),
            jax.ShapeDtypeStruct((4, COLS), f32),
        ],
        in_specs=vmem(11) + [in_hbm] * 3,
        out_specs=vmem(3),
        scratch_shapes=[
            pltpu.VMEM((2, FIELDS, ROWS, COLS), f32),
            pltpu.VMEM((PAIRS * ROWS, COLS), f32),
            pltpu.VMEM((MEMBERS, COLS), f32),
            pltpu.VMEM((DIRS, COLS), f32),
            pltpu.VMEM((1, COLS), jnp.int32),
            pltpu.VMEM((1, COLS), f32),
            pltpu.VMEM((1, COLS), f32),
            pltpu.SemaphoreType.DMA((3,)),
        ]
        + [pltpu.VMEM(level_shape.shape, f32)] * 4
        + [pltpu.VMEM(strip_level.shape, f32)] * 4,
        compiler_params=small,
    )(here, *interior, first, second, jnp.broadcast_to(obs_count, (1, COLS)), index, value, weight)

    fine = min(16, lon_tiles)
    index = [[lon * lat_tiles + lat for lat in range(lat_tiles)] for lon in range(lon_tiles)]
    near = [
        [index[base + k][lat] for k in range(fine)] for base in range(0, lon_tiles, fine) for lat in range(lat_tiles)
    ]
    far = [[index[lon][lat] for lon in range(k, lon_tiles, fine) for lat in range(lat_tiles)] for k in range(fine)]
    part = jnp.sum(all_parts(part, near), axis=0)
    parts = all_parts(part, far)
    analysis, spread = pl.pallas_call(
        analysis_kernel,
        out_shape=[jax.ShapeDtypeStruct((PAIRS * ROWS, COLS), f32), jax.ShapeDtypeStruct((MEMBERS, MEMBERS), f32)],
        in_specs=vmem(3),
        out_specs=vmem(2),
        scratch_shapes=[pltpu.VMEM((DIRS, COLS), f32)],
        compiler_params=small,
    )(parts, modes, mean)
    return analysis.reshape(sample_collection.shape), spread


def solution(mesh):
    return jax.shard_map(
        on_device,
        mesh=mesh,
        in_specs=(
            P(None, None, "lat", "lon"),
            P("lat", "lon", None),
            P("lat", "lon"),
            P("lat", "lon", None),
            P("lat", "lon", None),
        ),
        out_specs=(P(None, None, "lat", "lon"), P()),
        check_vma=False,
    )
```

```python
import math

import jax
import jax.numpy as jnp
from jax import lax
from jax.experimental import pallas as pl
from jax.experimental.pallas import tpu as pltpu
from jax.sharding import PartitionSpec as P


DIRS = 16
MEMBERS = 17
FIELDS = 6
PAIRS = MEMBERS * FIELDS
SUBSTEPS = 4
RIM = 4
ROWS = 8
COLS = 128
CELLS = FIELDS * ROWS * COLS
TILES = FIELDS * ROWS
HOME = 12
DEEP = 32
GROUP = 2
STRIPS = FIELDS + 1
MSG_ROWS = (PAIRS + STRIPS) * RIM

time_step = 0.15
depth_top = 4.0
depth_low = 6.0
forget = 0.9
highest = lax.Precision.HIGHEST
f32 = jnp.float32


def iota(shape, axis):
    return lax.broadcasted_iota(jnp.int32, shape, axis)


def vmem(count):
    return [pl.BlockSpec(memory_space=pltpu.VMEM)] * count


def pack_kernel(x_hbm, strip_ref, x_ref, sem):
    move = pltpu.make_async_copy(x_hbm, x_ref.at[:, HOME : HOME + ROWS, :], sem)
    move.start()
    move.wait()
    lane = iota((ROWS, COLS), 1)
    for strip in range(STRIPS):
        total = jnp.zeros((ROWS, COLS), f32)
        for place in range(DIRS if strip < FIELDS else FIELDS):
            pair = place * FIELDS + strip if strip < FIELDS else DIRS * FIELDS + place
            block = x_ref[pair, HOME : HOME + ROWS, :]
            moved = pltpu.roll(block, 8 * place, 1) if place else block
            mask = ((lane - (8 * place - 4)) & (COLS - 1)) < 8
            total = jnp.where(mask, moved, total)
        strip_ref[strip] = total


def message_kernel(x_ref, strip1_ref, strip2_ref, own_ref, first_ref, second_ref):
    even_lon = (lax.axis_index("lon") & 1) == 0
    even_lat = (lax.axis_index("lat") & 1) == 0
    eastern = (iota((ROWS, COLS), 1) & 7) < RIM

    def merge(first_is_east):
        east, west = (strip1_ref, strip2_ref) if first_is_east else (strip2_ref, strip1_ref)
        for strip in range(STRIPS):
            own_ref[strip] = jnp.where(eastern, east[strip], west[strip])

    pl.when(even_lon)(lambda: merge(True))
    pl.when(jnp.logical_not(even_lon))(lambda: merge(False))

    def rows_out(north_first):
        north, south = (first_ref, second_ref) if north_first else (second_ref, first_ref)
        for pair in range(PAIRS):
            at = slice(RIM * pair, RIM * (pair + 1))
            north[at, :] = x_ref[pair, HOME + RIM : HOME + ROWS, :]
            south[at, :] = x_ref[pair, HOME : HOME + RIM, :]
        for strip in range(STRIPS):
            at = slice(RIM * (PAIRS + strip), RIM * (PAIRS + strip + 1))
            north[at, :] = own_ref[strip, RIM:ROWS, :]
            south[at, :] = own_ref[strip, 0:RIM, :]

    pl.when(even_lat)(lambda: rows_out(True))
    pl.when(jnp.logical_not(even_lat))(lambda: rows_out(False))


def layer(thick, zonal, merid, slope_x, slope_y, depth, turn):
    (h, hE, hW, hN, hS), (u, uE, uW, uN, uS), (v, vE, vW, vN, vS) = thick, zonal, merid
    half = 0.5 * time_step
    flux = ((depth + hE) * uE - (depth + hW) * uW) + ((depth + hN) * vN - (depth + hS) * vS)
    h_new = 0.25 * ((hE + hW) + (hN + hS)) - half * flux
    u_new = 0.25 * ((uE + uW) + (uN + uS)) - (
        half * (u * (uE - uW) + v * (uN - uS) + slope_x) - turn * v
    )
    v_new = 0.25 * ((vE + vW) + (vN + vS)) - (
        half * (u * (vE - vW) + v * (vN - vS) + slope_y) + turn * u
    )
    return h_new, u_new, v_new


def advance(stencil, turn):
    top, low = stencil[0], stencil[3]
    top_x, top_y = top[1] - top[2], top[3] - top[4]
    low_x, low_y = low[1] - low[2], low[3] - low[4]
    sum_x, sum_y = top_x + low_x, top_y + low_y
    upper = layer(top, stencil[1], stencil[2], sum_x, sum_y, depth_top, turn)
    lower = layer(low, stencil[4], stencil[5], sum_x + 0.5 * low_x, sum_y + 0.5 * low_y, depth_low, turn)
    return upper + lower


def split(value):
    high = value.astype(jnp.bfloat16)
    rest = value - high.astype(f32)
    middle = rest.astype(jnp.bfloat16)
    return high, middle, (rest - middle.astype(f32)).astype(jnp.bfloat16)


def sweep(read, emit, read_strip, emit_strip, inner, turn):
    lane = iota((ROWS, COLS), 1)

    def members_step(members, which, shifts):
        stencils = []
        for member, shift in zip(members, shifts):
            stencil = []
            for field in range(FIELDS):
                c, n, s = read(member * FIELDS + field)
                beyond = read_strip(which, field)[0]
                if shift is not None:
                    beyond = pltpu.roll(beyond, COLS - shift, 1)
                e = pltpu.roll(jnp.where(lane == 0, beyond, c), COLS - 1, 1)
                w = pltpu.roll(jnp.where(lane == COLS - 1, beyond, c), 1, 1)
                stencil.append((c, e, w, n, s))
            stencils.append(stencil)
        if emit_strip is not None:
            for field in range(FIELDS):
                if shifts[0] is None:
                    inner[which, field] = stencils[0][field][0]
                    continue
                total = inner[which, field]
                for shift, stencil in zip(shifts, stencils):
                    edge = ((lane - shift + 1) & (COLS - 1)) < 2
                    total = jnp.where(edge, pltpu.roll(stencil[field][0], shift, 1), total)
                inner[which, field] = total
        for member, stencil in zip(members, stencils):
            for field, value in enumerate(advance(stencil, turn)):
                emit(member * FIELDS + field, value)

    def group_step(index, carry):
        for part in range(2):
            members = [GROUP * (2 * index + part) + k for k in range(GROUP)]
            members_step(members, 0, [8 * member for member in members])
        return carry

    lax.fori_loop(0, DIRS // GROUP // 2, group_step, 0)
    members_step([DIRS], 1, [None])
    if emit_strip is None:
        return
    for which in range(2):
        stencil = []
        for field in range(FIELDS):
            c, n, s = read_strip(which, field)
            beyond = inner[which, field]
            e = pltpu.roll(jnp.where((lane & 7) == 0, beyond, c), COLS - 1, 1)
            w = pltpu.roll(jnp.where((lane & 7) == 7, beyond, c), 1, 1)
            stencil.append((c, e, w, n, s))
        for field, value in enumerate(advance(stencil, turn)):
            emit_strip(which, field, value)


def row_terms(first, second):
    lats = lax.axis_size("lat")
    sub = iota((ROWS, COLS), 0)
    row = jnp.where(sub < RIM, sub + first, sub - RIM + second) + lax.axis_index("lat") * ROWS
    inside = (row >= 0) & (row < lats * ROWS)
    turn = time_step * (0.5 * (2.0 * (row.astype(f32) + 0.5) / float(lats * ROWS) - 1.0))
    return inside, turn


def spread_strips(blocks, strips, first, last, at):
    for strip in range(STRIPS):
        for field in range(FIELDS) if strip == FIELDS else [strip]:
            block = blocks(strip)
            if strip == FIELDS and field:
                block = pltpu.roll(block, COLS - 8 * field, 1)
            strips[strip // FIELDS, field, at : at + last - first, :] = block[first:last, :]


def interior_kernel(x_ref, own_ref, *refs):
    levels, strip_levels, inner = [x_ref, *refs[0:3]], refs[3:7], refs[7]
    _, turn = row_terms(0, RIM)
    spread_strips(lambda strip: own_ref[strip], strip_levels[0], 0, ROWS, HOME)
    for step in range(SUBSTEPS - 1):
        old, fresh = levels[step], levels[step + 1]
        old_strips, fresh_strips = strip_levels[step], strip_levels[step + 1]

        def read(pair, old=old):
            return [old[pair, HOME + d : HOME + d + ROWS, :] for d in (0, 1, -1)]

        def emit(pair, value, fresh=fresh):
            fresh[pair, HOME : HOME + ROWS, :] = value

        def read_strip(which, field, old_strips=old_strips):
            return [old_strips[which, field, HOME + d : HOME + d + ROWS, :] for d in (0, 1, -1)]

        def emit_strip(which, field, value, fresh_strips=fresh_strips):
            fresh_strips[which, field, HOME : HOME + ROWS, :] = value

        sweep(read, emit, read_strip, emit_strip, inner, turn)


def forecast_kernel(*refs):
    levels, strip_levels = refs[0:4], refs[4:8]
    first_ref, second_ref, count_ref, index_hbm, value_hbm, weight_hbm = refs[8:14]
    modes_ref, mean_ref, pay_ref, inner, final, seen, gram, index_ref, value_ref, weight_ref, sems = refs[14:25]
    states, strips = refs[25:29], refs[29:33]
    moves = [
        pltpu.make_async_copy(source, target, sems.at[place])
        for place, (source, target) in enumerate(
            [(index_hbm, index_ref), (value_hbm, value_ref), (weight_hbm, weight_ref)]
        )
    ]
    for move in moves:
        move.start()
    lats = lax.axis_size("lat")
    even = (lax.axis_index("lat") & 1) == 0

    def rows_in(north_first):
        north, south = (first_ref, second_ref) if north_first else (second_ref, first_ref)
        for pair in range(PAIRS):
            at = slice(RIM * pair, RIM * (pair + 1))
            states[0][pair, HOME - RIM : HOME, :] = south[at, :]
            states[0][pair, HOME + ROWS : HOME + ROWS + RIM, :] = north[at, :]

        def corner(rows):
            return lambda strip: rows[RIM * (PAIRS + strip) : RIM * (PAIRS + strip + 1), :]

        spread_strips(corner(south), strips[0], 0, RIM, HOME - RIM)
        spread_strips(corner(north), strips[0], 0, RIM, HOME + ROWS)

    pl.when(even)(lambda: rows_in(True))
    pl.when(jnp.logical_not(even))(lambda: rows_in(False))
    home = slice(HOME, HOME + ROWS)
    for source, target in zip(levels, states):
        for pair in range(PAIRS):
            target[pair, home, :] = source[pair, home, :]
    for source, target in zip(strip_levels, strips):
        for which in range(2):
            for field in range(FIELDS):
                target[which, field, home, :] = source[which, field, home, :]

    upper = iota((ROWS, COLS), 0) < RIM
    for step in range(SUBSTEPS - 1):
        low, high = step - 3, 7 - step
        inside, turn = row_terms(low, high)

        def both(ref, *at, low=low, high=high):
            return [
                jnp.where(
                    upper,
                    ref[(*at, slice(HOME + low + d, HOME + low + d + ROWS), slice(None))],
                    ref[(*at, slice(HOME + high - RIM + d, HOME + high + RIM + d), slice(None))],
                )
                for d in (0, 1, -1)
            ]

        def put(ref, value, *at, low=low, high=high, inside=inside):
            value = jnp.where(inside, value, 0.0)
            ref[(*at, slice(HOME + low, HOME + low + RIM), slice(None))] = value[0:RIM, :]
            ref[(*at, slice(HOME + high, HOME + high + RIM), slice(None))] = value[RIM:ROWS, :]

        sweep(
            lambda pair, step=step, both=both: both(states[step], pair),
            lambda pair, value, step=step, put=put: put(states[step + 1], value, pair),
            lambda which, field, step=step, both=both: both(strips[step], which, field),
            lambda which, field, value, step=step, put=put: put(strips[step + 1], value, which, field),
            inner,
            turn,
        )

    def own_rows(ref, *at):
        return [ref[(*at, slice(HOME + d, HOME + d + ROWS), slice(None))] for d in (0, 1, -1)]

    def finish(pair, value):
        final[pl.ds(pl.multiple_of(pair * ROWS, ROWS), ROWS), :] = value

    sweep(
        lambda pair: own_rows(states[3], pair),
        finish,
        lambda which, field: own_rows(strips[3], which, field),
        None,
        inner,
        row_terms(0, RIM)[1],
    )

    sub8 = iota((ROWS, COLS), 0)
    for move in moves:
        move.wait()
    cell = index_ref[...]
    column = jnp.broadcast_to(cell & (COLS - 1), (ROWS, COLS))
    at_row = jnp.broadcast_to(lax.shift_right_logical(cell, 7), (ROWS, COLS)) == sub8
    def block(member, field):
        at = (member * FIELDS + field) * ROWS
        return final[at : at + ROWS, :]

    for member in range(MEMBERS):
        surface = block(member, 0) + block(member, 3)
        picked = jnp.take_along_axis(surface, column, axis=1)
        seen[member : member + 1, :] = jnp.sum(jnp.where(at_row, picked, 0.0), axis=0, keepdims=True)

    for field in range(FIELDS):
        total = block(0, field)
        for member in range(1, MEMBERS):
            total = total + block(member, field)
        mean_ref[ROWS * field : ROWS * (field + 1), :] = total * (1.0 / MEMBERS)
    for tile in range(TILES):
        span = slice(COLS * tile, COLS * (tile + 1))
        parts = split(final[pl.ds(tile, DIRS, stride=TILES), :] - mean_ref[tile : tile + 1, :])
        for place, part in enumerate(parts):
            modes_ref[DIRS * place : DIRS * (place + 1), span] = part

    stack = modes_ref[...]
    blocks = lax.dot_general(stack, stack, (((1,), (1,)), ((), ())), preferred_element_type=f32)
    rows3 = blocks[0:DIRS, :] + (blocks[DIRS : 2 * DIRS, :] + blocks[2 * DIRS :, :])
    mode_gram = rows3[:, 0:DIRS] + (rows3[:, DIRS : 2 * DIRS] + rows3[:, 2 * DIRS :])

    observed = seen[...]
    obs_mean = jnp.sum(observed, axis=0, keepdims=True) * (1.0 / MEMBERS)
    anomaly = observed[0:DIRS, :] - obs_mean
    innovation = value_ref[...] - obs_mean
    live = (iota((1, COLS), 1) < count_ref[...]).astype(f32)
    weighted = anomaly * (weight_ref[...] * live / float(COLS * lats * lax.axis_size("lon")))
    obs_gram = lax.dot_general(
        weighted, anomaly, (((1,), (1,)), ((), ())), precision=highest, preferred_element_type=f32
    )
    obs_proj = jnp.sum(weighted * innovation, axis=1, keepdims=True)
    row, col = iota((DIRS, DIRS), 0), iota((DIRS, DIRS), 1)
    gram[...] = jnp.zeros((DIRS, COLS), f32)
    gram[:, 0:DIRS] = jnp.where(row < col, obs_gram, mode_gram)
    gram[:, DIRS : DIRS + 1] = jnp.sum(jnp.where(row == col, obs_gram, 0.0), axis=1, keepdims=True)
    gram[:, DIRS + 1 : DIRS + 2] = obs_proj
    packed = gram[0:4, :]
    for quarter in range(1, 4):
        packed = packed + pltpu.roll(gram[4 * quarter : 4 * quarter + 4, :], 32 * quarter, 1)
    pay_ref[...] = packed


def analysis_kernel(parts_ref, modes_ref, mean_ref, out_ref, spread_ref, gram):
    packed = jnp.sum(parts_ref[...], axis=0)
    for quarter in range(4):
        gram[4 * quarter : 4 * quarter + 4, :] = (
            pltpu.roll(packed, COLS - 32 * quarter, 1) if quarter else packed
        )
    joined = gram[...]
    row, col = iota((DIRS, DIRS), 0), iota((DIRS, DIRS), 1)
    square = joined[:, 0:DIRS]
    upper = jnp.where(row < col, square, 0.0)
    lower = jnp.where(row > col, square, 0.0)
    mode_gram = jnp.where(row == col, square, 0.0) + (lower + lower.T)
    obs_gram = jnp.where(row == col, joined[:, DIRS : DIRS + 1], 0.0) + (upper + upper.T)
    precision = obs_gram + (DIRS / forget) * (jnp.where(row == col, 1.0, 0.0) - 1.0 / MEMBERS)
    sub, lane = iota((DIRS, COLS), 0), iota((DIRS, COLS), 1)
    copies = 6 * DIRS
    gram[:, copies : copies + DIRS] = precision
    gram[:, copies + DIRS : copies + DIRS + 1] = joined[:, DIRS + 1 : DIRS + 2]
    unit = jnp.where((lane & (DIRS - 1)) == sub, 1.0, 0.0)
    work = jnp.where(lane < copies, unit, gram[...])
    work = jnp.where(lane <= copies + DIRS, work, 0.0)
    for first in range(0, DIRS, 16):
        pivots = range(first, first + 16)
        columns = [jnp.broadcast_to(work[:, copies + p : copies + p + 1], (DIRS, COLS)) for p in pivots]
        rows = []
        for k, pivot in enumerate(pivots):
            column, pivot_row = columns[k], work[pivot : pivot + 1, :]
            for q in range(k):
                factor = columns[q][pivot : pivot + 1, :]
                column = column - columns[q] * factor
                pivot_row = pivot_row - factor * rows[q]
            value = column[pivot : pivot + 1, :]
            inverse = lax.rsqrt(value)
            inverse = inverse * (1.5 - 0.5 * value * inverse * inverse)
            columns[k] = column * inverse
            rows.append(pivot_row * inverse)
        below = work
        for k in range(16):
            below = below - columns[k] * rows[k]
        work = jnp.where(sub >= first + 16, below, work)
        for k, pivot in enumerate(pivots):
            work = jnp.where(sub == pivot, rows[k], work)
    inverse_factor = work[:, :copies]
    solved = work[:, copies + DIRS : copies + DIRS + 1]
    weights = jnp.sum(solved * inverse_factor, axis=0, keepdims=True)
    spare = (math.sqrt(MEMBERS) - 1.0) / DIRS
    scale = math.sqrt(DIRS)
    sums = jnp.sum(inverse_factor, axis=0, keepdims=True)
    rotation_t = jnp.concatenate(
        [
            scale * inverse_factor + (scale * (spare - 1.0) / MEMBERS) * sums,
            (-scale * (1.0 + DIRS * spare) / MEMBERS) * sums,
        ],
        axis=0,
    )
    coefficient_t = rotation_t + weights
    high, middle, low = split(coefficient_t)
    place = iota((MEMBERS, copies), 1)
    stack = jnp.where(place < 3 * DIRS, high.astype(f32), jnp.where(place < 5 * DIRS, middle.astype(f32), low.astype(f32)))
    stack = stack.astype(jnp.bfloat16)
    for field in range(FIELDS):
        span = slice(field * ROWS * COLS, (field + 1) * ROWS * COLS)
        parts = jnp.concatenate(
            [modes_ref[:, span], modes_ref[0 : 2 * DIRS, span], modes_ref[0:DIRS, span]], axis=0
        )
        update = jnp.dot(stack, parts, preferred_element_type=f32)
        for row_here in range(ROWS):
            tile = field * ROWS + row_here
            values = update[:, COLS * row_here : COLS * (row_here + 1)] + mean_ref[tile : tile + 1, :]
            out_ref[pl.ds(tile, DIRS, stride=TILES), :] = values[0:DIRS, :]
            out_ref[DIRS * TILES + tile : DIRS * TILES + tile + 1, :] = values[DIRS:MEMBERS, :]
    rotation_t = rotation_t[:, 0:DIRS]
    half_way = jnp.dot(rotation_t, mode_gram, precision=highest, preferred_element_type=f32)
    spread = lax.dot_general(
        half_way, rotation_t, (((1,), (1,)), ((), ())), precision=highest, preferred_element_type=f32
    )
    spread_ref[...] = spread / float(CELLS * lax.axis_size("lat") * lax.axis_size("lon"))


def neighbours(axis, parity, wrap):
    count = lax.axis_size(axis)
    pairs = [(i, i + 1) for i in range(parity, count - 1, 2)]
    if wrap and parity:
        pairs.append((count - 1, 0))
    return pairs + [(j, i) for i, j in pairs]


def all_parts(part, groups):
    count = len(groups[0])
    return lax.all_to_all(
        jnp.broadcast_to(part[None], (count,) + part.shape), ("lon", "lat"), 0, 0, axis_index_groups=groups
    )


def on_device(sample_collection, obs_index, obs_count, obs_value, obs_weight):
    lat_tiles, lon_tiles = lax.axis_size("lat"), lax.axis_size("lon")
    small = pltpu.CompilerParams(vmem_limit_bytes=20 * 2**20)
    in_hbm = pl.BlockSpec(memory_space=pltpu.HBM)
    blocks, index, value, weight = [
        pltpu.with_memory_space_constraint(array, pltpu.HBM)
        for array in (
            sample_collection.reshape(PAIRS, ROWS, COLS),
            obs_index.reshape(1, COLS),
            obs_value.reshape(1, COLS),
            obs_weight.reshape(1, COLS),
        )
    ]
    strips_shape = jax.ShapeDtypeStruct((STRIPS, ROWS, COLS), f32)
    level_shape = jax.ShapeDtypeStruct((PAIRS, DEEP, COLS), f32)
    strip_level = jax.ShapeDtypeStruct((2, FIELDS, DEEP, COLS), f32)
    strip_msg, here = pl.pallas_call(
        pack_kernel,
        out_shape=[strips_shape, level_shape],
        in_specs=[in_hbm],
        out_specs=vmem(2),
        scratch_shapes=[pltpu.SemaphoreType.DMA],
        compiler_params=small,
    )(blocks)
    strip1 = lax.ppermute(strip_msg, "lon", neighbours("lon", 0, True))
    strip2 = lax.ppermute(strip_msg, "lon", neighbours("lon", 1, True))
    own_strip, first_msg, second_msg = pl.pallas_call(
        message_kernel,
        out_shape=[strips_shape] + [jax.ShapeDtypeStruct((MSG_ROWS, COLS), f32)] * 2,
        in_specs=vmem(3),
        out_specs=vmem(3),
        compiler_params=small,
    )(here, strip1, strip2)
    first = lax.ppermute(first_msg, "lat", neighbours("lat", 0, False))
    second = lax.ppermute(second_msg, "lat", neighbours("lat", 1, False))
    interior = pl.pallas_call(
        interior_kernel,
        out_shape=[level_shape] * 3 + [strip_level] * 4,
        in_specs=vmem(2),
        out_specs=vmem(7),
        scratch_shapes=[pltpu.VMEM((2, FIELDS, ROWS, COLS), f32)],
        compiler_params=small,
        cost_estimate=pl.CostEstimate(flops=40_000_000, bytes_accessed=2_000_000, transcendentals=0),
    )(here, own_strip)

    modes, mean, part = pl.pallas_call(
        forecast_kernel,
        out_shape=[
            jax.ShapeDtypeStruct((3 * DIRS, CELLS), jnp.bfloat16),
            jax.ShapeDtypeStruct((TILES, COLS), f32),
            jax.ShapeDtypeStruct((4, COLS), f32),
        ],
        in_specs=vmem(11) + [in_hbm] * 3,
        out_specs=vmem(3),
        scratch_shapes=[
            pltpu.VMEM((2, FIELDS, ROWS, COLS), f32),
            pltpu.VMEM((PAIRS * ROWS, COLS), f32),
            pltpu.VMEM((MEMBERS, COLS), f32),
            pltpu.VMEM((DIRS, COLS), f32),
            pltpu.VMEM((1, COLS), jnp.int32),
            pltpu.VMEM((1, COLS), f32),
            pltpu.VMEM((1, COLS), f32),
            pltpu.SemaphoreType.DMA((3,)),
        ]
        + [pltpu.VMEM(level_shape.shape, f32)] * 4
        + [pltpu.VMEM(strip_level.shape, f32)] * 4,
        compiler_params=small,
    )(here, *interior, first, second, jnp.broadcast_to(obs_count, (1, COLS)), index, value, weight)

    fine = min(16, lon_tiles)
    index = [[lon * lat_tiles + lat for lat in range(lat_tiles)] for lon in range(lon_tiles)]
    near = [
        [index[base + k][lat] for k in range(fine)] for base in range(0, lon_tiles, fine) for lat in range(lat_tiles)
    ]
    far = [[index[lon][lat] for lon in range(k, lon_tiles, fine) for lat in range(lat_tiles)] for k in range(fine)]
    part = jnp.sum(all_parts(part, far), axis=0)
    parts = all_parts(part, near)
    analysis, spread = pl.pallas_call(
        analysis_kernel,
        out_shape=[jax.ShapeDtypeStruct((PAIRS * ROWS, COLS), f32), jax.ShapeDtypeStruct((MEMBERS, MEMBERS), f32)],
        in_specs=vmem(3),
        out_specs=vmem(2),
        scratch_shapes=[pltpu.VMEM((DIRS, COLS), f32)],
        compiler_params=small,
    )(parts, modes, mean)
    return analysis.reshape(sample_collection.shape), spread


def solution(mesh):
    return jax.shard_map(
        on_device,
        mesh=mesh,
        in_specs=(
            P(None, None, "lat", "lon"),
            P("lat", "lon", None),
            P("lat", "lon"),
            P("lat", "lon", None),
            P("lat", "lon", None),
        ),
        out_specs=(P(None, None, "lat", "lon"), P()),
        check_vma=False,
    )
```

```python
import math

import jax
import jax.numpy as jnp
from jax import lax
from jax.experimental import pallas as pl
from jax.experimental.pallas import tpu as pltpu
from jax.sharding import PartitionSpec as P


DIRS = 16
MEMBERS = 17
FIELDS = 6
PAIRS = MEMBERS * FIELDS
SUBSTEPS = 4
RIM = 4
ROWS = 8
COLS = 128
CELLS = FIELDS * ROWS * COLS
TILES = FIELDS * ROWS
HOME = 12
DEEP = 32
GROUP = 2
STRIPS = FIELDS + 1
MSG_ROWS = (PAIRS + STRIPS) * RIM

time_step = 0.15
depth_top = 4.0
depth_low = 6.0
forget = 0.9
highest = lax.Precision.HIGHEST
f32 = jnp.float32


def iota(shape, axis):
    return lax.broadcasted_iota(jnp.int32, shape, axis)


def vmem(count):
    return [pl.BlockSpec(memory_space=pltpu.VMEM)] * count


def pack_kernel(x_hbm, strip_ref, x_ref, sem):
    move = pltpu.make_async_copy(x_hbm, x_ref.at[:, HOME : HOME + ROWS, :], sem)
    move.start()
    move.wait()
    lane = iota((ROWS, COLS), 1)
    for strip in range(STRIPS):
        total = jnp.zeros((ROWS, COLS), f32)
        for place in range(DIRS if strip < FIELDS else FIELDS):
            pair = place * FIELDS + strip if strip < FIELDS else DIRS * FIELDS + place
            block = x_ref[pair, HOME : HOME + ROWS, :]
            moved = pltpu.roll(block, 8 * place, 1) if place else block
            mask = ((lane - (8 * place - 4)) & (COLS - 1)) < 8
            total = jnp.where(mask, moved, total)
        strip_ref[strip] = total


def message_kernel(x_ref, strip1_ref, strip2_ref, own_ref, first_ref, second_ref):
    even_lon = (lax.axis_index("lon") & 1) == 0
    even_lat = (lax.axis_index("lat") & 1) == 0
    eastern = (iota((ROWS, COLS), 1) & 7) < RIM

    def merge(first_is_east):
        east, west = (strip1_ref, strip2_ref) if first_is_east else (strip2_ref, strip1_ref)
        for strip in range(STRIPS):
            own_ref[strip] = jnp.where(eastern, east[strip], west[strip])

    pl.when(even_lon)(lambda: merge(True))
    pl.when(jnp.logical_not(even_lon))(lambda: merge(False))

    def rows_out(north_first):
        north, south = (first_ref, second_ref) if north_first else (second_ref, first_ref)
        for pair in range(PAIRS):
            at = slice(RIM * pair, RIM * (pair + 1))
            north[at, :] = x_ref[pair, HOME + RIM : HOME + ROWS, :]
            south[at, :] = x_ref[pair, HOME : HOME + RIM, :]
        for strip in range(STRIPS):
            at = slice(RIM * (PAIRS + strip), RIM * (PAIRS + strip + 1))
            north[at, :] = own_ref[strip, RIM:ROWS, :]
            south[at, :] = own_ref[strip, 0:RIM, :]

    pl.when(even_lat)(lambda: rows_out(True))
    pl.when(jnp.logical_not(even_lat))(lambda: rows_out(False))


def layer(thick, zonal, merid, slope_x, slope_y, depth, turn):
    (h, hE, hW, hN, hS), (u, uE, uW, uN, uS), (v, vE, vW, vN, vS) = thick, zonal, merid
    half = 0.5 * time_step
    flux = ((depth + hE) * uE - (depth + hW) * uW) + ((depth + hN) * vN - (depth + hS) * vS)
    h_new = 0.25 * ((hE + hW) + (hN + hS)) - half * flux
    u_new = 0.25 * ((uE + uW) + (uN + uS)) - (
        half * (u * (uE - uW) + v * (uN - uS) + slope_x) - turn * v
    )
    v_new = 0.25 * ((vE + vW) + (vN + vS)) - (
        half * (u * (vE - vW) + v * (vN - vS) + slope_y) + turn * u
    )
    return h_new, u_new, v_new


def advance(stencil, turn):
    top, low = stencil[0], stencil[3]
    top_x, top_y = top[1] - top[2], top[3] - top[4]
    low_x, low_y = low[1] - low[2], low[3] - low[4]
    sum_x, sum_y = top_x + low_x, top_y + low_y
    upper = layer(top, stencil[1], stencil[2], sum_x, sum_y, depth_top, turn)
    lower = layer(low, stencil[4], stencil[5], sum_x + 0.5 * low_x, sum_y + 0.5 * low_y, depth_low, turn)
    return upper + lower


def split(value):
    high = value.astype(jnp.bfloat16)
    rest = value - high.astype(f32)
    middle = rest.astype(jnp.bfloat16)
    return high, middle, (rest - middle.astype(f32)).astype(jnp.bfloat16)


def sweep(read, emit, read_strip, emit_strip, inner, turn):
    lane = iota((ROWS, COLS), 1)

    def members_step(members, which, shifts):
        stencils = []
        for member, shift in zip(members, shifts):
            stencil = []
            for field in range(FIELDS):
                c, n, s = read(member * FIELDS + field)
                beyond = read_strip(which, field)[0]
                if shift is not None:
                    beyond = pltpu.roll(beyond, COLS - shift, 1)
                e = pltpu.roll(jnp.where(lane == 0, beyond, c), COLS - 1, 1)
                w = pltpu.roll(jnp.where(lane == COLS - 1, beyond, c), 1, 1)
                stencil.append((c, e, w, n, s))
            stencils.append(stencil)
        if emit_strip is not None:
            for field in range(FIELDS):
                if shifts[0] is None:
                    inner[which, field] = stencils[0][field][0]
                    continue
                total = inner[which, field]
                for shift, stencil in zip(shifts, stencils):
                    edge = ((lane - shift + 1) & (COLS - 1)) < 2
                    total = jnp.where(edge, pltpu.roll(stencil[field][0], shift, 1), total)
                inner[which, field] = total
        for member, stencil in zip(members, stencils):
            for field, value in enumerate(advance(stencil, turn)):
                emit(member * FIELDS + field, value)

    def group_step(index, carry):
        for part in range(2):
            members = [GROUP * (2 * index + part) + k for k in range(GROUP)]
            members_step(members, 0, [8 * member for member in members])
        return carry

    lax.fori_loop(0, DIRS // GROUP // 2, group_step, 0)
    members_step([DIRS], 1, [None])
    if emit_strip is None:
        return
    for which in range(2):
        stencil = []
        for field in range(FIELDS):
            c, n, s = read_strip(which, field)
            beyond = inner[which, field]
            e = pltpu.roll(jnp.where((lane & 7) == 0, beyond, c), COLS - 1, 1)
            w = pltpu.roll(jnp.where((lane & 7) == 7, beyond, c), 1, 1)
            stencil.append((c, e, w, n, s))
        for field, value in enumerate(advance(stencil, turn)):
            emit_strip(which, field, value)


def row_terms(first, second):
    lats = lax.axis_size("lat")
    sub = iota((ROWS, COLS), 0)
    row = jnp.where(sub < RIM, sub + first, sub - RIM + second) + lax.axis_index("lat") * ROWS
    inside = (row >= 0) & (row < lats * ROWS)
    turn = time_step * (0.5 * (2.0 * (row.astype(f32) + 0.5) / float(lats * ROWS) - 1.0))
    return inside, turn


def spread_strips(blocks, strips, first, last, at):
    for strip in range(STRIPS):
        for field in range(FIELDS) if strip == FIELDS else [strip]:
            block = blocks(strip)
            if strip == FIELDS and field:
                block = pltpu.roll(block, COLS - 8 * field, 1)
            strips[strip // FIELDS, field, at : at + last - first, :] = block[first:last, :]


def interior_kernel(x_ref, own_ref, *refs):
    levels, strip_levels, inner = [x_ref, *refs[0:3]], refs[3:7], refs[7]
    _, turn = row_terms(0, RIM)
    spread_strips(lambda strip: own_ref[strip], strip_levels[0], 0, ROWS, HOME)
    for step in range(SUBSTEPS - 1):
        old, fresh = levels[step], levels[step + 1]
        old_strips, fresh_strips = strip_levels[step], strip_levels[step + 1]

        def read(pair, old=old):
            return [old[pair, HOME + d : HOME + d + ROWS, :] for d in (0, 1, -1)]

        def emit(pair, value, fresh=fresh):
            fresh[pair, HOME : HOME + ROWS, :] = value

        def read_strip(which, field, old_strips=old_strips):
            return [old_strips[which, field, HOME + d : HOME + d + ROWS, :] for d in (0, 1, -1)]

        def emit_strip(which, field, value, fresh_strips=fresh_strips):
            fresh_strips[which, field, HOME : HOME + ROWS, :] = value

        sweep(read, emit, read_strip, emit_strip, inner, turn)


def forecast_kernel(*refs):
    levels, strip_levels = refs[0:4], refs[4:8]
    first_ref, second_ref, count_ref, index_hbm, value_hbm, weight_hbm = refs[8:14]
    modes_ref, mean_ref, pay_ref, inner, final, seen, gram, index_ref, value_ref, weight_ref, sems = refs[14:25]
    states, strips = refs[25:29], refs[29:33]
    moves = [
        pltpu.make_async_copy(source, target, sems.at[place])
        for place, (source, target) in enumerate(
            [(index_hbm, index_ref), (value_hbm, value_ref), (weight_hbm, weight_ref)]
        )
    ]
    for move in moves:
        move.start()
    lats = lax.axis_size("lat")
    even = (lax.axis_index("lat") & 1) == 0

    def rows_in(north_first):
        north, south = (first_ref, second_ref) if north_first else (second_ref, first_ref)
        for pair in range(PAIRS):
            at = slice(RIM * pair, RIM * (pair + 1))
            states[0][pair, HOME - RIM : HOME, :] = south[at, :]
            states[0][pair, HOME + ROWS : HOME + ROWS + RIM, :] = north[at, :]

        def corner(rows):
            return lambda strip: rows[RIM * (PAIRS + strip) : RIM * (PAIRS + strip + 1), :]

        spread_strips(corner(south), strips[0], 0, RIM, HOME - RIM)
        spread_strips(corner(north), strips[0], 0, RIM, HOME + ROWS)

    pl.when(even)(lambda: rows_in(True))
    pl.when(jnp.logical_not(even))(lambda: rows_in(False))
    home = slice(HOME, HOME + ROWS)
    for source, target in zip(levels, states):
        for pair in range(PAIRS):
            target[pair, home, :] = source[pair, home, :]
    for source, target in zip(strip_levels, strips):
        for which in range(2):
            for field in range(FIELDS):
                target[which, field, home, :] = source[which, field, home, :]

    upper = iota((ROWS, COLS), 0) < RIM
    for step in range(SUBSTEPS - 1):
        low, high = step - 3, 7 - step
        inside, turn = row_terms(low, high)

        def both(ref, *at, low=low, high=high):
            return [
                jnp.where(
                    upper,
                    ref[(*at, slice(HOME + low + d, HOME + low + d + ROWS), slice(None))],
                    ref[(*at, slice(HOME + high - RIM + d, HOME + high + RIM + d), slice(None))],
                )
                for d in (0, 1, -1)
            ]

        def put(ref, value, *at, low=low, high=high, inside=inside):
            value = jnp.where(inside, value, 0.0)
            ref[(*at, slice(HOME + low, HOME + low + RIM), slice(None))] = value[0:RIM, :]
            ref[(*at, slice(HOME + high, HOME + high + RIM), slice(None))] = value[RIM:ROWS, :]

        sweep(
            lambda pair, step=step, both=both: both(states[step], pair),
            lambda pair, value, step=step, put=put: put(states[step + 1], value, pair),
            lambda which, field, step=step, both=both: both(strips[step], which, field),
            lambda which, field, value, step=step, put=put: put(strips[step + 1], value, which, field),
            inner,
            turn,
        )

    def own_rows(ref, *at):
        return [ref[(*at, slice(HOME + d, HOME + d + ROWS), slice(None))] for d in (0, 1, -1)]

    def finish(pair, value):
        final[pl.ds(pl.multiple_of(pair * ROWS, ROWS), ROWS), :] = value

    sweep(
        lambda pair: own_rows(states[3], pair),
        finish,
        lambda which, field: own_rows(strips[3], which, field),
        None,
        inner,
        row_terms(0, RIM)[1],
    )

    sub8 = iota((ROWS, COLS), 0)
    for move in moves:
        move.wait()
    cell = index_ref[...]
    column = jnp.broadcast_to(cell & (COLS - 1), (ROWS, COLS))
    at_row = jnp.broadcast_to(lax.shift_right_logical(cell, 7), (ROWS, COLS)) == sub8
    def block(member, field):
        at = (member * FIELDS + field) * ROWS
        return final[at : at + ROWS, :]

    for member in range(MEMBERS):
        surface = block(member, 0) + block(member, 3)
        picked = jnp.take_along_axis(surface, column, axis=1)
        seen[member : member + 1, :] = jnp.sum(jnp.where(at_row, picked, 0.0), axis=0, keepdims=True)

    for field in range(FIELDS):
        total = block(0, field)
        for member in range(1, MEMBERS):
            total = total + block(member, field)
        mean_ref[ROWS * field : ROWS * (field + 1), :] = total * (1.0 / MEMBERS)
    for tile in range(TILES):
        span = slice(COLS * tile, COLS * (tile + 1))
        parts = split(final[pl.ds(tile, DIRS, stride=TILES), :] - mean_ref[tile : tile + 1, :])
        for place, part in enumerate(parts):
            modes_ref[DIRS * place : DIRS * (place + 1), span] = part

    stack = modes_ref[...]
    blocks = lax.dot_general(stack, stack, (((1,), (1,)), ((), ())), preferred_element_type=f32)
    rows3 = blocks[0:DIRS, :] + (blocks[DIRS : 2 * DIRS, :] + blocks[2 * DIRS :, :])
    mode_gram = rows3[:, 0:DIRS] + (rows3[:, DIRS : 2 * DIRS] + rows3[:, 2 * DIRS :])

    observed = seen[...]
    obs_mean = jnp.sum(observed, axis=0, keepdims=True) * (1.0 / MEMBERS)
    anomaly = observed[0:DIRS, :] - obs_mean
    innovation = value_ref[...] - obs_mean
    live = (iota((1, COLS), 1) < count_ref[...]).astype(f32)
    weighted = anomaly * (weight_ref[...] * live / float(COLS * lats * lax.axis_size("lon")))
    obs_gram = lax.dot_general(
        weighted, anomaly, (((1,), (1,)), ((), ())), precision=highest, preferred_element_type=f32
    )
    obs_proj = jnp.sum(weighted * innovation, axis=1, keepdims=True)
    row, col = iota((DIRS, DIRS), 0), iota((DIRS, DIRS), 1)
    gram[...] = jnp.zeros((DIRS, COLS), f32)
    gram[:, 0:DIRS] = jnp.where(row < col, obs_gram, mode_gram)
    gram[:, DIRS : DIRS + 1] = jnp.sum(jnp.where(row == col, obs_gram, 0.0), axis=1, keepdims=True)
    gram[:, DIRS + 1 : DIRS + 2] = obs_proj
    packed = gram[0:4, :]
    for quarter in range(1, 4):
        packed = packed + pltpu.roll(gram[4 * quarter : 4 * quarter + 4, :], 32 * quarter, 1)
    pay_ref[...] = packed


def analysis_kernel(parts_ref, modes_ref, mean_ref, out_ref, spread_ref, gram):
    packed = jnp.sum(parts_ref[...], axis=0)
    for quarter in range(4):
        gram[4 * quarter : 4 * quarter + 4, :] = (
            pltpu.roll(packed, COLS - 32 * quarter, 1) if quarter else packed
        )
    joined = gram[...]
    row, col = iota((DIRS, DIRS), 0), iota((DIRS, DIRS), 1)
    square = joined[:, 0:DIRS]
    upper = jnp.where(row < col, square, 0.0)
    lower = jnp.where(row > col, square, 0.0)
    mode_gram = jnp.where(row == col, square, 0.0) + (lower + lower.T)
    obs_gram = jnp.where(row == col, joined[:, DIRS : DIRS + 1], 0.0) + (upper + upper.T)
    precision = obs_gram + (DIRS / forget) * (jnp.where(row == col, 1.0, 0.0) - 1.0 / MEMBERS)
    sub, lane = iota((DIRS, COLS), 0), iota((DIRS, COLS), 1)
    copies = 6 * DIRS
    gram[:, copies : copies + DIRS] = precision
    gram[:, copies + DIRS : copies + DIRS + 1] = joined[:, DIRS + 1 : DIRS + 2]
    unit = jnp.where((lane & (DIRS - 1)) == sub, 1.0, 0.0)
    work = jnp.where(lane < copies, unit, gram[...])
    work = jnp.where(lane <= copies + DIRS, work, 0.0)
    for first in range(0, DIRS, 16):
        pivots = range(first, first + 16)
        columns = [jnp.broadcast_to(work[:, copies + p : copies + p + 1], (DIRS, COLS)) for p in pivots]
        rows = []
        for k, pivot in enumerate(pivots):
            column, pivot_row = columns[k], work[pivot : pivot + 1, :]
            for q in range(k):
                factor = columns[q][pivot : pivot + 1, :]
                column = column - columns[q] * factor
                pivot_row = pivot_row - factor * rows[q]
            value = column[pivot : pivot + 1, :]
            inverse = lax.rsqrt(value)
            inverse = inverse * (1.5 - 0.5 * value * inverse * inverse)
            columns[k] = column * inverse
            rows.append(pivot_row * inverse)
        below = work
        for k in range(16):
            below = below - columns[k] * rows[k]
        work = jnp.where(sub >= first + 16, below, work)
        for k, pivot in enumerate(pivots):
            work = jnp.where(sub == pivot, rows[k], work)
    inverse_factor = work[:, :copies]
    solved = work[:, copies + DIRS : copies + DIRS + 1]
    weights = jnp.sum(solved * inverse_factor, axis=0, keepdims=True)
    spare = (math.sqrt(MEMBERS) - 1.0) / DIRS
    scale = math.sqrt(DIRS)
    sums = jnp.sum(inverse_factor, axis=0, keepdims=True)
    rotation_t = jnp.concatenate(
        [
            scale * inverse_factor + (scale * (spare - 1.0) / MEMBERS) * sums,
            (-scale * (1.0 + DIRS * spare) / MEMBERS) * sums,
        ],
        axis=0,
    )
    coefficient_t = rotation_t + weights
    high, middle, low = split(coefficient_t)
    place = iota((MEMBERS, copies), 1)
    stack = jnp.where(place < 3 * DIRS, high.astype(f32), jnp.where(place < 5 * DIRS, middle.astype(f32), low.astype(f32)))
    stack = stack.astype(jnp.bfloat16)
    for field in range(FIELDS):
        span = slice(field * ROWS * COLS, (field + 1) * ROWS * COLS)
        parts = jnp.concatenate(
            [modes_ref[:, span], modes_ref[0 : 2 * DIRS, span], modes_ref[0:DIRS, span]], axis=0
        )
        update = jnp.dot(stack, parts, preferred_element_type=f32)
        for row_here in range(ROWS):
            tile = field * ROWS + row_here
            out_ref[pl.ds(tile, MEMBERS, stride=TILES), :] = (
                update[:, COLS * row_here : COLS * (row_here + 1)] + mean_ref[tile : tile + 1, :]
            )
    rotation_t = rotation_t[:, 0:DIRS]
    half_way = jnp.dot(rotation_t, mode_gram, precision=highest, preferred_element_type=f32)
    spread = lax.dot_general(
        half_way, rotation_t, (((1,), (1,)), ((), ())), precision=highest, preferred_element_type=f32
    )
    spread_ref[...] = spread / float(CELLS * lax.axis_size("lat") * lax.axis_size("lon"))


def neighbours(axis, parity, wrap):
    count = lax.axis_size(axis)
    pairs = [(i, i + 1) for i in range(parity, count - 1, 2)]
    if wrap and parity:
        pairs.append((count - 1, 0))
    return pairs + [(j, i) for i, j in pairs]


def all_parts(part, groups):
    count = len(groups[0])
    return lax.all_to_all(
        jnp.broadcast_to(part[None], (count,) + part.shape), ("lon", "lat"), 0, 0, axis_index_groups=groups
    )


def on_device(sample_collection, obs_index, obs_count, obs_value, obs_weight):
    lat_tiles, lon_tiles = lax.axis_size("lat"), lax.axis_size("lon")
    small = pltpu.CompilerParams(vmem_limit_bytes=20 * 2**20)
    in_hbm = pl.BlockSpec(memory_space=pltpu.HBM)
    blocks, index, value, weight = [
        pltpu.with_memory_space_constraint(array, pltpu.HBM)
        for array in (
            sample_collection.reshape(PAIRS, ROWS, COLS),
            obs_index.reshape(1, COLS),
            obs_value.reshape(1, COLS),
            obs_weight.reshape(1, COLS),
        )
    ]
    strips_shape = jax.ShapeDtypeStruct((STRIPS, ROWS, COLS), f32)
    level_shape = jax.ShapeDtypeStruct((PAIRS, DEEP, COLS), f32)
    strip_level = jax.ShapeDtypeStruct((2, FIELDS, DEEP, COLS), f32)
    strip_msg, here = pl.pallas_call(
        pack_kernel,
        out_shape=[strips_shape, level_shape],
        in_specs=[in_hbm],
        out_specs=vmem(2),
        scratch_shapes=[pltpu.SemaphoreType.DMA],
        compiler_params=small,
    )(blocks)
    strip1 = lax.ppermute(strip_msg, "lon", neighbours("lon", 0, True))
    strip2 = lax.ppermute(strip_msg, "lon", neighbours("lon", 1, True))
    own_strip, first_msg, second_msg = pl.pallas_call(
        message_kernel,
        out_shape=[strips_shape] + [jax.ShapeDtypeStruct((MSG_ROWS, COLS), f32)] * 2,
        in_specs=vmem(3),
        out_specs=vmem(3),
        compiler_params=small,
    )(here, strip1, strip2)
    first = lax.ppermute(first_msg, "lat", neighbours("lat", 0, False))
    second = lax.ppermute(second_msg, "lat", neighbours("lat", 1, False))
    interior = pl.pallas_call(
        interior_kernel,
        out_shape=[level_shape] * 3 + [strip_level] * 4,
        in_specs=vmem(2),
        out_specs=vmem(7),
        scratch_shapes=[pltpu.VMEM((2, FIELDS, ROWS, COLS), f32)],
        compiler_params=small,
        cost_estimate=pl.CostEstimate(flops=40_000_000, bytes_accessed=2_000_000, transcendentals=0),
    )(here, own_strip)

    modes, mean, part = pl.pallas_call(
        forecast_kernel,
        out_shape=[
            jax.ShapeDtypeStruct((3 * DIRS, CELLS), jnp.bfloat16),
            jax.ShapeDtypeStruct((TILES, COLS), f32),
            jax.ShapeDtypeStruct((4, COLS), f32),
        ],
        in_specs=vmem(11) + [in_hbm] * 3,
        out_specs=vmem(3),
        scratch_shapes=[
            pltpu.VMEM((2, FIELDS, ROWS, COLS), f32),
            pltpu.VMEM((PAIRS * ROWS, COLS), f32),
            pltpu.VMEM((MEMBERS, COLS), f32),
            pltpu.VMEM((DIRS, COLS), f32),
            pltpu.VMEM((1, COLS), jnp.int32),
            pltpu.VMEM((1, COLS), f32),
            pltpu.VMEM((1, COLS), f32),
            pltpu.SemaphoreType.DMA((3,)),
        ]
        + [pltpu.VMEM(level_shape.shape, f32)] * 4
        + [pltpu.VMEM(strip_level.shape, f32)] * 4,
        compiler_params=small,
    )(here, *interior, first, second, jnp.broadcast_to(obs_count, (1, COLS)), index, value, weight)

    index = [[lon * lat_tiles + lat for lat in range(lat_tiles)] for lon in range(lon_tiles)]
    near = [
        [index[base + k][lat] for k in range(2) for lat in range(start, lat_tiles, 2)]
        for base in range(0, lon_tiles, 2)
        for start in range(2)
    ]
    far = [
        [index[lon][base + k] for lon in range(start, lon_tiles, 2) for k in range(2)]
        for base in range(0, lat_tiles, 2)
        for start in range(2)
    ]
    part = jnp.sum(all_parts(part, near), axis=0)
    parts = all_parts(part, far)
    analysis, spread = pl.pallas_call(
        analysis_kernel,
        out_shape=[jax.ShapeDtypeStruct((PAIRS * ROWS, COLS), f32), jax.ShapeDtypeStruct((MEMBERS, MEMBERS), f32)],
        in_specs=vmem(3),
        out_specs=vmem(2),
        scratch_shapes=[pltpu.VMEM((DIRS, COLS), f32)],
        compiler_params=small,
    )(parts, modes, mean)
    return analysis.reshape(sample_collection.shape), spread


def solution(mesh):
    return jax.shard_map(
        on_device,
        mesh=mesh,
        in_specs=(
            P(None, None, "lat", "lon"),
            P("lat", "lon", None),
            P("lat", "lon"),
            P("lat", "lon", None),
            P("lat", "lon", None),
        ),
        out_specs=(P(None, None, "lat", "lon"), P()),
        check_vma=False,
    )
```
